32 devices in a mesh: dp: 8 (over y, x, core), tensor: 4 (over z).
Axes of the slice: x: 2, y: 2, z: 4, core: 2. Of those that a mesh axis runs over, the one named last changes fastest.
Arguments:
- tokens: bfloat16 [8, 1024, 1280], P('dp', 'tensor'), may hold values from -6 to 6
- lengths: int32 [8], P('dp'), may hold values from 256 to 1024, as said below
- cotangent: bfloat16 [8, 1024, 1280], P('dp', 'tensor'), may hold values from -6 to 6
- ln1_gain: bfloat16 [1280], P('dp'), may hold values from 0.099609375 to 1.8984375
- ln1_bias: bfloat16 [1280], P('dp'), may hold values from -3 to 3
- query_weight: bfloat16 [1280, 1280], P('dp', 'tensor'), may hold values from -0.25 to 0.25
- query_bias: bfloat16 [1280], P('tensor'), may hold values from -3 to 3
- key_weight: bfloat16 [1280, 1280], P('dp', 'tensor'), may hold values from -0.25 to 0.25
- value_weight: bfloat16 [1280, 1280], P('dp', 'tensor'), may hold values from -0.15625 to 0.15625
- value_bias: bfloat16 [1280], P('tensor'), may hold values from -3 to 3
- out_weight: bfloat16 [1280, 1280], P('dp', 'tensor'), may hold values from -1.25 to 1.25
- out_bias: bfloat16 [1280], P('dp'), may hold values from -3 to 3
- ln2_gain: bfloat16 [1280], P('dp'), may hold values from 0.099609375 to 1.8984375
- ln2_bias: bfloat16 [1280], P('dp'), may hold values from -3 to 3
- up_weight: bfloat16 [1280, 5120], P('dp', 'tensor'), may hold values from -0.15625 to 0.15625
- up_bias: bfloat16 [5120], P('tensor'), may hold values from -3 to 3
- down_weight: bfloat16 [1280, 5120], P('dp', 'tensor'), may hold values from -0.25 to 0.25
- down_bias: bfloat16 [1280], P('dp'), may hold values from -3 to 3
Outputs:
- output: bfloat16 [8, 1024, 1280], P('dp', 'tensor')
- tokens_grad: float32 [8, 1024, 1280], P('dp', 'tensor')
- ln1_gain_grad: float32 [1280], P('dp')
- ln1_bias_grad: float32 [1280], P('dp')
- query_weight_grad: float32 [1280, 1280], P('dp', 'tensor')
- query_bias_grad: float32 [1280], P('tensor')
- key_weight_grad: float32 [1280, 1280], P('dp', 'tensor')
- value_weight_grad: float32 [1280, 1280], P('dp', 'tensor')
- value_bias_grad: float32 [1280], P('tensor')
- out_weight_grad: float32 [1280, 1280], P('dp', 'tensor')
- out_bias_grad: float32 [1280], P('dp')
- ln2_gain_grad: float32 [1280], P('dp')
- ln2_bias_grad: float32 [1280], P('dp')
- up_weight_grad: float32 [1280, 5120], P('dp', 'tensor')
- up_bias_grad: float32 [5120], P('tensor')
- down_weight_grad: float32 [1280, 5120], P('dp', 'tensor')
- down_bias_grad: float32 [1280], P('dp')
The draws below stay inside these ranges and needn't reach their ends.
Inputs may be any that keep to these rules, and one draw needn't show every extreme that they name: `lengths`: positions of a clip at or past its length are padding and are masked as keys; some clip has exactly 1024 valid positions and some exactly 256.
All inputs are finite; a program needn't handle non-finite values.
Results may differ from the reference program's by a relative error of at most 0.02.
Values may be sent and summed in bfloat16 or wider, within the bound.
No kernel may reach another device: no remote copies, remote signals or barrier semaphores. Data moves between devices by JAX's collectives and lax.ppermute only.
A program may use at most 128 MiB of HBM per device.

```python
import jax
import jax.numpy as jnp
from jax import lax

D = 1280
HEADS = 16
HEAD_DIM = 80
FF = 5120
SEQ = 1024
CLIPS = 8
N_TENSOR = 4


def draw_lengths(key, part):
    drawn = jax.random.randint(key, (CLIPS,), SEQ // 4, SEQ + 1, dtype=jnp.int32)
    drawn = drawn.at[0].set(SEQ)
    return drawn.at[1].set(SEQ // 4)


def level_of(key, dims, cuts, low, largest):
    level, own = 1.0, jax.random.fold_in(key, 6)
    for axis_at, shards_of in cuts:
        draws = jnp.exp(jax.random.uniform(jax.random.fold_in(own, axis_at), (shards_of,), jnp.float32, low / len(cuts), largest / len(cuts)))
        level = level * jnp.repeat(draws, dims[axis_at] // shards_of).reshape([-1 if axis == axis_at else 1 for axis in range(len(dims))])
    return level


def bell_draw(own_key, extent, deviation, most, pieces=(), kind=jnp.bfloat16):
    values = deviation * jax.random.normal(own_key, extent, jnp.float32)
    if pieces:
        values = values * level_of(own_key, extent, pieces, -0.22, 0.18)
    return jnp.clip(values, -most, most).astype(kind)


def setup_inputs(seed: int = 0) -> dict:
    keys = jax.random.split(jax.random.key(seed), 19)
    return {
        "tokens": bell_draw(keys[0], (CLIPS, SEQ, D), 1.0, 6.0, ((0, 8), (1, 4))),
        "lengths": draw_lengths(jax.random.fold_in(keys[18], 71), 0),
        "cotangent": bell_draw(keys[2], (CLIPS, SEQ, D), 1.0, 6.0, ((0, 8), (1, 4))),
        "ln1_gain": jnp.clip(1.0 + 0.18 * jax.random.normal(keys[3], (D,), jnp.float32), 0.099609375, 1.8984375).astype(jnp.bfloat16),
        "ln1_bias": bell_draw(keys[4], (D,), 0.5, 3.0, ((0, 8),)),
        "query_weight": bell_draw(keys[5], (D, D), (D // 2) ** -0.5, 0.25, ((0, 8), (1, 4))),
        "query_bias": bell_draw(keys[6], (D,), 0.5, 3.0, ((0, 4),)),
        "key_weight": bell_draw(keys[7], (D, D), (D // 2) ** -0.5, 0.25, ((0, 8), (1, 4))),
        "value_weight": bell_draw(keys[8], (D, D), D ** -0.5, 0.15625, ((0, 8), (1, 4))),
        "value_bias": bell_draw(keys[9], (D,), 0.5, 3.0, ((0, 4),)),
        "out_weight": bell_draw(keys[10], (D, D), (max(D // 64, 1)) ** -0.5, 1.25, ((0, 8), (1, 4))),
        "out_bias": bell_draw(keys[11], (D,), 0.5, 3.0, ((0, 8),)),
        "ln2_gain": jnp.clip(1.0 + 0.18 * jax.random.normal(keys[12], (D,), jnp.float32), 0.099609375, 1.8984375).astype(jnp.bfloat16),
        "ln2_bias": bell_draw(keys[13], (D,), 0.5, 3.0, ((0, 8),)),
        "up_weight": bell_draw(keys[14], (D, FF), D ** -0.5, 0.15625, ((0, 8), (1, 4))),
        "up_bias": bell_draw(keys[15], (FF,), 0.5, 3.0, ((0, 4),)),
        "down_weight": bell_draw(keys[16], (D, FF), (FF // 8) ** -0.5, 0.25, ((0, 8), (1, 4))),
        "down_bias": bell_draw(keys[17], (D,), 0.5, 3.0, ((0, 8),)),
    }


@jax.custom_vjp
def low(v):
    return lax.optimization_barrier(v.astype(jnp.bfloat16)).astype(jnp.float32)

@jax.custom_vjp
def low_back(v):
    return v

def low_keep(v):
    return (low(v), None)

def low_pass(kept, grad):
    return (grad,)

def back_keep(v):
    return (v, None)

def back_low(kept, grad):
    return (low(grad),)
low.defvjp(low_keep, low_pass)
low_back.defvjp(back_keep, back_low)
masked_score = -1e+30

def layer_norm(values, gain, shift):
    centre = values - lax.optimization_barrier(jnp.mean(values, axis=-1, keepdims=True))
    spread = lax.optimization_barrier(jnp.mean(centre * centre, axis=-1, keepdims=True))
    return centre * lax.rsqrt(spread + 1e-05) * gain + shift

def one_clip(params, clip_rows, length):
    ln1_gain, ln1_bias, query_weight, query_bias, key_weight, value_weight, value_bias, out_weight, out_bias, ln2_gain, ln2_bias, up_weight, up_bias, down_weight, down_bias = params
    exact = lax.Precision.HIGHEST
    width = D // N_TENSOR
    ff_width = FF // N_TENSOR
    normed = low(layer_norm(clip_rows, ln1_gain, ln1_bias))
    query_parts = []
    key_parts = []
    value_parts = []
    for group in range(N_TENSOR):
        lower = group * width
        upper = lower + width
        normed_copy = low_back(normed)
        query_parts.append(low(low_back(jnp.dot(normed_copy, query_weight[:, lower:upper], precision=exact) + query_bias[lower:upper])))
        key_parts.append(low(low_back(jnp.dot(normed_copy, key_weight[:, lower:upper], precision=exact))))
        value_parts.append(low(low_back(jnp.dot(normed_copy, value_weight[:, lower:upper], precision=exact) + value_bias[lower:upper])))
    queries = jnp.concatenate(query_parts, axis=1)
    keyed = jnp.concatenate(key_parts, axis=1)
    valued = jnp.concatenate(value_parts, axis=1)
    shaped = (SEQ, HEADS, HEAD_DIM)
    scores = low_back(HEAD_DIM ** (-0.5) * jnp.einsum('qhe,khe->hqk', queries.reshape(shaped), keyed.reshape(shaped), precision=exact))
    valid = lax.broadcasted_iota(jnp.int32, (SEQ,), 0) < length
    scores = jnp.where(valid[None, None, :], scores, masked_score)
    top = lax.optimization_barrier(jnp.max(scores, axis=-1, keepdims=True))
    expo = jnp.exp(scores - top)
    probs = expo / lax.optimization_barrier(jnp.sum(expo, axis=-1, keepdims=True))
    context = low(low_back(jnp.einsum('hqk,khe->qhe', low(probs), valued.reshape(shaped), precision=exact))).reshape(SEQ, D)
    attended = jnp.zeros((SEQ, D), jnp.float32)
    for group in range(N_TENSOR):
        lower = group * width
        upper = lower + width
        attended = attended + low(jnp.dot(context[:, lower:upper], out_weight[:, lower:upper].T, precision=exact))
    attended = low_back(attended)
    middle = clip_rows + attended + out_bias
    normed_two = low(layer_norm(middle, ln2_gain, ln2_bias))
    mixed = jnp.zeros((SEQ, D), jnp.float32)
    for group in range(N_TENSOR):
        lower = group * ff_width
        upper = lower + ff_width
        normed_copy = low_back(normed_two)
        hidden_pre = low_back(jnp.dot(normed_copy, up_weight[:, lower:upper], precision=exact) + up_bias[lower:upper])
        hidden = low(jax.nn.gelu(hidden_pre, approximate=False))
        mixed = mixed + low(jnp.dot(hidden, down_weight[:, lower:upper].T, precision=exact))
    mixed = low_back(mixed)
    return middle + mixed + down_bias

def reference(tokens, lengths, cotangent, ln1_gain, ln1_bias, query_weight, query_bias, key_weight, value_weight, value_bias, out_weight, out_bias, ln2_gain, ln2_bias, up_weight, up_bias, down_weight, down_bias):
    params = tuple((item.astype(jnp.float32) for item in (ln1_gain, ln1_bias, query_weight, query_bias, key_weight, value_weight, value_bias, out_weight, out_bias, ln2_gain, ln2_bias, up_weight, up_bias, down_weight, down_bias)))
    start = tokens.astype(jnp.float32)
    clip_step = jax.checkpoint(one_clip)

    def forward(weights, rows):
        return lax.map(lambda item: clip_step(weights, item[0], item[1]), (rows, lengths))
    result, pullback = jax.vjp(forward, params, start)
    weight_grads, tokens_grad = pullback(cotangent.astype(jnp.float32))
    return (result.astype(jnp.bfloat16), tokens_grad, weight_grads[0], weight_grads[1], weight_grads[2], weight_grads[3], weight_grads[4], weight_grads[5], weight_grads[6], weight_grads[7], weight_grads[8], weight_grads[9], weight_grads[10], weight_grads[11], weight_grads[12], weight_grads[13], weight_grads[14])
```

```python
import jax
import jax.numpy as jnp
from jax import lax
from jax.sharding import PartitionSpec as P

HEAD_DIM = 80


masked_score = -1e30


def layer_norm(values, gain, shift):
    centre = values - jnp.mean(values, axis=-1, keepdims=True)
    spread = jnp.mean(centre * centre, axis=-1, keepdims=True)
    return centre * lax.rsqrt(spread + 1e-05) * gain + shift


SEATS = 4
SLOT = 256
CORE, ACROSS, ALONG = 1, 2, 4


def dot(left, right, dims):
    return lax.dot_general(
        left, right, (((dims[0],), (dims[1],)), ((), ())), preferred_element_type=jnp.float32
    )


def swap(values, bits):
    size = lax.axis_size("dp")
    return lax.ppermute(values, "dp", [(k, k ^ bits) for k in range(size)])


def plane_swap(values, bits, planes):
    return lax.ppermute(values, "tensor", [(k, k ^ bits) for k in range(planes)])


def at_index(stack, index):
    return lax.dynamic_index_in_dim(stack, index, 0, keepdims=False)


def to_plane(rows, seat, plane, planes):
    parts = rows.reshape(SEATS, -1, rows.shape[1])
    got = jnp.stack(
        [at_index(parts, seat)]
        + [swap(at_index(parts, seat ^ r), r << 1) for r in range(1, SEATS)]
    )
    turn = seat ^ plane
    return jnp.concatenate(
        [at_index(got, turn)]
        + [plane_swap(at_index(got, turn ^ k), k, planes) for k in range(1, planes)]
    )


def from_plane(rows, seat, plane, planes):
    parts = rows.reshape(planes, -1, rows.shape[1])
    got = jnp.stack([parts[0]] + [plane_swap(parts[k], k, planes) for k in range(1, planes)])
    turn = seat ^ plane
    back = jnp.stack(
        [at_index(got, turn)]
        + [swap(at_index(got, turn ^ r), r << 1) for r in range(1, SEATS)]
    )
    return jnp.concatenate([at_index(back, s ^ seat) for s in range(SEATS)])


def plane_gather(own):
    half = own.shape[0] // 2
    a, b = own[:half], own[half:]
    across_a, along_b = swap(a, ACROSS), swap(b, ALONG)
    across_b, along_a = swap(b, ACROSS), swap(a, ALONG)
    far_a, far_b = swap(across_a, ALONG), swap(along_b, ACROSS)
    return jnp.concatenate([a, b, across_a, across_b, along_a, along_b, far_a, far_b])


def plane_scatter(terms):
    rows = terms.shape[0] // SEATS
    half = rows // 2

    def piece(k):
        return terms[k * half : (k + 1) * half].astype(jnp.float32)

    def low(v):
        return v.astype(jnp.bfloat16)

    far_a = swap(low(piece(6)), ACROSS).astype(jnp.float32)
    far_b = swap(low(piece(7)), ALONG).astype(jnp.float32)
    across_a = swap(low(piece(2)), ACROSS).astype(jnp.float32)
    along_b = swap(low(piece(5)), ALONG).astype(jnp.float32)
    along_a = swap(low(piece(4) + far_a), ALONG).astype(jnp.float32)
    across_b = swap(low(piece(3) + far_b), ACROSS).astype(jnp.float32)
    return jnp.concatenate([piece(0) + across_a + along_a, piece(1) + across_b + along_b])


def seat_exchange(pieces, seat):
    got = jnp.stack(
        [at_index(pieces, seat)]
        + [swap(at_index(pieces, seat ^ r), r << 1) for r in range(1, SEATS)]
    )
    return jnp.concatenate([at_index(got, s ^ seat) for s in range(SEATS)])


def with_row(rows, row):
    return jnp.concatenate([rows, jnp.broadcast_to(row, (16, row.shape[0]))])


def line_gather(own, planes, plane):
    above = below = own
    ups, downs = [], []
    for t in range(1, planes):
        above = lax.ppermute(above, "tensor", [(j, j + 1) for j in range(t - 1, planes - 1)])
        below = lax.ppermute(below, "tensor", [(j, j - 1) for j in range(1, planes - t + 1)])
        ups.append(above)
        downs.append(below)
    return [own] + [
        jnp.where(plane >= t, ups[t - 1], downs[planes - t - 1]) for t in range(1, planes)
    ]


def line_scatter(chunks, planes):
    up = down = jnp.zeros((), jnp.float32)
    wide = [c.astype(jnp.float32) for c in chunks]
    for step in range(1, planes):
        k = planes - step
        up = lax.ppermute(
            (wide[planes - k] + up).astype(jnp.bfloat16),
            "tensor",
            [(j, j + 1) for j in range(step)],
        ).astype(jnp.float32)
        down = lax.ppermute(
            (wide[k] + down).astype(jnp.bfloat16),
            "tensor",
            [(planes - 1 - j, planes - 2 - j) for j in range(step)],
        ).astype(jnp.float32)
    return wide[0] + up + down


def both_cores(half, core, rows_of):
    other = swap(half, CORE)
    mine = half.reshape(SEATS, 1, rows_of, -1)
    other = other.reshape(SEATS, 1, rows_of, -1)
    first = jnp.where(core == 0, mine, other)
    second = jnp.where(core == 0, other, mine)
    return jnp.concatenate([first, second], axis=1).reshape(2 * SEATS * rows_of, -1)


def core_scatter(full, core, rows_of):
    paired = full.reshape(SEATS, 2, rows_of, -1)
    kept = lax.dynamic_index_in_dim(paired, core, 1, keepdims=False)
    given = lax.dynamic_index_in_dim(paired, 1 - core, 1, keepdims=False)
    return kept.astype(jnp.float32) + swap(given, CORE).astype(jnp.float32)


def weights_home(chunks, core, seat, rows_of, planes):
    kept = [core_scatter(c, core, rows_of).astype(jnp.bfloat16) for c in chunks]
    owned = line_scatter(kept, planes).astype(jnp.bfloat16)
    return jnp.stack(
        [at_index(owned, seat)]
        + [swap(at_index(owned, seat ^ r), r << 1) for r in range(1, SEATS)]
    )


def norm_back(values, gain, grad):
    mean = jnp.mean(values, axis=-1, keepdims=True)
    centre = values - mean
    root = lax.rsqrt(jnp.mean(centre * centre, axis=-1, keepdims=True) + 1e-05)
    unit = centre * root
    scaled = grad * gain
    part = root * (
        scaled
        - jnp.mean(scaled, axis=-1, keepdims=True)
        - unit * jnp.mean(scaled * unit, axis=-1, keepdims=True)
    )
    return part, jnp.sum(grad * unit, axis=0), jnp.sum(grad, axis=0)


def masked_scores(query_part, key_rows, valid, scale):
    scores = (
        jnp.einsum("qhe,khe->hqk", query_part, key_rows, preferred_element_type=jnp.float32) * scale
    )
    return jnp.where(valid[None, None, :], scores, masked_score)


def attend_clip(query_rows, key_rows, value_rows, valid, blocks):
    seq, heads = (query_rows.shape[0], query_rows.shape[1])
    scale = HEAD_DIM ** (-0.5)
    query_blocks = query_rows.reshape(blocks, seq // blocks, heads, HEAD_DIM)

    def one_block(query_part):
        scores = masked_scores(query_part, key_rows, valid, scale)
        top = jnp.max(scores, axis=-1, keepdims=True)
        expo = jnp.exp(scores - top)
        total = jnp.sum(expo, axis=-1, keepdims=True)
        probs = (expo / total).astype(jnp.bfloat16)
        context = jnp.einsum(
            "hqk,khe->qhe", probs, value_rows, preferred_element_type=jnp.float32
        ).astype(jnp.bfloat16)
        return (context, (top + jnp.log(total))[..., 0])

    context, log_total = lax.map(one_block, query_blocks)
    return (context.reshape(seq, heads, HEAD_DIM), log_total)


def attend_back(query_rows, key_rows, value_rows, context_grad, log_total, valid, blocks):
    seq, heads = (query_rows.shape[0], query_rows.shape[1])
    scale = HEAD_DIM ** (-0.5)
    query_blocks = query_rows.reshape(blocks, seq // blocks, heads, HEAD_DIM)
    grad_blocks = context_grad.reshape(blocks, seq // blocks, heads, HEAD_DIM)

    def one_block(carry, inputs):
        key_acc, value_acc = carry
        query_part, grad_part, lse_part = inputs
        scores = masked_scores(query_part, key_rows, valid, scale)
        probs = jnp.exp(scores - lse_part[..., None])
        value_acc = value_acc + jnp.einsum(
            "hqk,qhe->khe",
            probs.astype(jnp.bfloat16),
            grad_part,
            preferred_element_type=jnp.float32,
        )
        prob_grad = jnp.einsum(
            "qhe,khe->hqk", grad_part, value_rows, preferred_element_type=jnp.float32
        )
        centred = prob_grad - jnp.sum(probs * prob_grad, axis=-1, keepdims=True)
        score_grad = (probs * centred).astype(jnp.bfloat16)
        query_grad = (
            jnp.einsum("hqk,khe->qhe", score_grad, key_rows, preferred_element_type=jnp.float32)
            * scale
        )
        key_acc = (
            key_acc
            + jnp.einsum("hqk,qhe->khe", score_grad, query_part, preferred_element_type=jnp.float32)
            * scale
        )
        return ((key_acc, value_acc), query_grad.astype(jnp.bfloat16))

    zeros = jnp.zeros((seq, heads, HEAD_DIM), jnp.float32)
    (key_acc, value_acc), query_grad = lax.scan(
        one_block, (zeros, zeros), (query_blocks, grad_blocks, log_total)
    )
    return (
        query_grad.reshape(seq, heads, HEAD_DIM),
        key_acc.astype(jnp.bfloat16),
        value_acc.astype(jnp.bfloat16),
    )


def forward_pass(tokens, lengths, weights):
    (
        ln1_gain,
        ln1_bias,
        query_weight,
        query_bias,
        key_weight,
        value_weight,
        value_bias,
        out_weight,
        out_bias,
        ln2_gain,
        ln2_bias,
        up_weight,
        up_bias,
        down_weight,
        down_bias,
    ) = weights
    query_full, key_full, value_full, out_full, gain_one, bias_one, out_shift = (
        lax.all_gather(query_weight, "dp", axis=0, tiled=True),
        lax.all_gather(key_weight, "dp", axis=0, tiled=True),
        lax.all_gather(value_weight, "dp", axis=0, tiled=True),
        lax.all_gather(out_weight, "dp", axis=0, tiled=True),
        lax.all_gather(ln1_gain, "dp", axis=0, tiled=True),
        lax.all_gather(ln1_bias, "dp", axis=0, tiled=True),
        lax.all_gather(out_bias, "dp", axis=0, tiled=True),
    )
    gain_one = gain_one.astype(jnp.float32)
    bias_one = bias_one.astype(jnp.float32)
    rows = tokens.astype(jnp.float32)
    normed = layer_norm(rows, gain_one, bias_one).astype(jnp.bfloat16)
    normed_all = lax.all_gather(normed, "tensor", axis=1, tiled=True)
    clips, seq = (normed_all.shape[0], normed_all.shape[1])
    heads = query_full.shape[1] // HEAD_DIM
    blocks = seq // 512
    shaped = (clips, seq, heads, HEAD_DIM)
    queries = (
        (
            jnp.einsum("csd,dh->csh", normed_all, query_full, preferred_element_type=jnp.float32)
            + query_bias.astype(jnp.float32)
        )
        .astype(jnp.bfloat16)
        .reshape(shaped)
    )
    keyed = (
        jnp.einsum("csd,dh->csh", normed_all, key_full, preferred_element_type=jnp.float32)
        .astype(jnp.bfloat16)
        .reshape(shaped)
    )
    valued = (
        (
            jnp.einsum("csd,dh->csh", normed_all, value_full, preferred_element_type=jnp.float32)
            + value_bias.astype(jnp.float32)
        )
        .astype(jnp.bfloat16)
        .reshape(shaped)
    )

    def clip_attend(item):
        valid = lax.broadcasted_iota(jnp.int32, (seq,), 0) < item[3]
        return attend_clip(item[0], item[1], item[2], valid, blocks)

    context, log_total = lax.map(clip_attend, (queries, keyed, valued, lengths))
    context = context.reshape(clips, seq, heads * HEAD_DIM)
    attn_terms = jnp.einsum("csh,dh->csd", context, out_full, preferred_element_type=jnp.float32)
    attended = lax.psum_scatter(
        attn_terms.astype(jnp.bfloat16), "tensor", scatter_dimension=1, tiled=True
    ).astype(jnp.float32)
    middle = rows + attended + out_shift.astype(jnp.float32)
    up_full, down_full, gain_two, bias_two, down_shift = (
        lax.all_gather(up_weight, "dp", axis=0, tiled=True),
        lax.all_gather(down_weight, "dp", axis=0, tiled=True),
        lax.all_gather(ln2_gain, "dp", axis=0, tiled=True),
        lax.all_gather(ln2_bias, "dp", axis=0, tiled=True),
        lax.all_gather(down_bias, "dp", axis=0, tiled=True),
    )
    gain_two = gain_two.astype(jnp.float32)
    bias_two = bias_two.astype(jnp.float32)
    normed_two = layer_norm(middle, gain_two, bias_two).astype(jnp.bfloat16)
    normed_two_all = lax.all_gather(normed_two, "tensor", axis=1, tiled=True)
    hidden_pre = jnp.einsum(
        "csd,df->csf", normed_two_all, up_full, preferred_element_type=jnp.float32
    ) + up_bias.astype(jnp.float32)
    hidden = jax.nn.gelu(hidden_pre, approximate=False).astype(jnp.bfloat16)
    mlp_terms = jnp.einsum("csf,df->csd", hidden, down_full, preferred_element_type=jnp.float32)
    mixed = lax.psum_scatter(
        mlp_terms.astype(jnp.bfloat16), "tensor", scatter_dimension=1, tiled=True
    ).astype(jnp.float32)
    output = middle + mixed + down_shift.astype(jnp.float32)
    return {
        "output": output,
        "rows": rows,
        "normed_all": normed_all,
        "queries": queries,
        "keyed": keyed,
        "valued": valued,
        "context": context,
        "log_total": log_total,
        "middle": middle,
        "normed_two_all": normed_two_all,
        "hidden_pre": hidden_pre,
        "hidden": hidden,
        "query_full": query_full,
        "key_full": key_full,
        "value_full": value_full,
        "out_full": out_full,
        "up_full": up_full,
        "down_full": down_full,
        "gain_one": gain_one,
        "bias_one": bias_one,
        "gain_two": gain_two,
        "bias_two": bias_two,
        "blocks": blocks,
    }


def local(
    tokens,
    lengths,
    cotangent,
    ln1_gain,
    ln1_bias,
    query_weight,
    query_bias,
    key_weight,
    value_weight,
    value_bias,
    out_weight,
    out_bias,
    ln2_gain,
    ln2_bias,
    up_weight,
    up_bias,
    down_weight,
    down_bias,
):
    weights = (
        ln1_gain,
        ln1_bias,
        query_weight,
        query_bias,
        key_weight,
        value_weight,
        value_bias,
        out_weight,
        out_bias,
        ln2_gain,
        ln2_bias,
        up_weight,
        up_bias,
        down_weight,
        down_bias,
    )
    saved = forward_pass(tokens, lengths, weights)
    blocks = saved["blocks"]
    grad_out = cotangent.astype(jnp.float32)
    down_shift_grad = jnp.sum(grad_out, axis=(0, 1))
    grad_out_all = lax.all_gather(cotangent, "tensor", axis=1, tiled=True)
    down_grad = jnp.einsum(
        "csd,csf->df", grad_out_all, saved["hidden"], preferred_element_type=jnp.float32
    )
    hidden_grad = jnp.einsum(
        "csd,df->csf", grad_out_all, saved["down_full"], preferred_element_type=jnp.float32
    )
    gelu_pull = jax.vjp(lambda pre: jax.nn.gelu(pre, approximate=False), saved["hidden_pre"])[1]
    pre_grad = gelu_pull(hidden_grad)[0].astype(jnp.bfloat16)
    up_shift_grad = jnp.sum(pre_grad, axis=(0, 1), dtype=jnp.float32)
    up_grad = jnp.einsum(
        "csd,csf->df", saved["normed_two_all"], pre_grad, preferred_element_type=jnp.float32
    )
    up_grad_shard, down_grad_shard = (
        lax.psum_scatter(
            up_grad.astype(jnp.bfloat16), "dp", scatter_dimension=0, tiled=True
        ).astype(jnp.float32),
        lax.psum_scatter(
            down_grad.astype(jnp.bfloat16), "dp", scatter_dimension=0, tiled=True
        ).astype(jnp.float32),
    )
    normed_two_terms = jnp.einsum(
        "csf,df->csd", pre_grad, saved["up_full"], preferred_element_type=jnp.float32
    )
    normed_two_grad = lax.psum_scatter(
        normed_two_terms.astype(jnp.bfloat16), "tensor", scatter_dimension=1, tiled=True
    ).astype(jnp.float32)
    norm_pull = jax.vjp(layer_norm, saved["middle"], saved["gain_two"], saved["bias_two"])[1]
    middle_part, gain_two_grad, bias_two_grad = norm_pull(normed_two_grad)
    middle_grad = grad_out + middle_part
    out_shift_grad = jnp.sum(middle_grad, axis=(0, 1))
    middle_all = lax.all_gather(middle_grad.astype(jnp.bfloat16), "tensor", axis=1, tiled=True)
    out_grad = jnp.einsum(
        "csd,csh->dh", middle_all, saved["context"], preferred_element_type=jnp.float32
    )
    context_grad = jnp.einsum(
        "csd,dh->csh", middle_all, saved["out_full"], preferred_element_type=jnp.float32
    ).astype(jnp.bfloat16)
    queries = saved["queries"]
    clips, seq, heads = (queries.shape[0], queries.shape[1], queries.shape[2])

    def clip_back(item):
        valid = lax.broadcasted_iota(jnp.int32, (seq,), 0) < item[5]
        return attend_back(item[0], item[1], item[2], item[3], item[4], valid, blocks)

    query_grad, key_grad, value_grad = lax.map(
        clip_back,
        (
            queries,
            saved["keyed"],
            saved["valued"],
            context_grad.reshape(clips, seq, heads, HEAD_DIM),
            saved["log_total"],
            lengths,
        ),
    )
    flat = (clips, seq, heads * HEAD_DIM)
    query_grad = query_grad.reshape(flat)
    key_grad = key_grad.reshape(flat)
    value_grad = value_grad.reshape(flat)
    normed_all = saved["normed_all"]
    query_weight_grad = jnp.einsum(
        "csd,csh->dh", normed_all, query_grad, preferred_element_type=jnp.float32
    )
    key_weight_grad = jnp.einsum(
        "csd,csh->dh", normed_all, key_grad, preferred_element_type=jnp.float32
    )
    value_weight_grad = jnp.einsum(
        "csd,csh->dh", normed_all, value_grad, preferred_element_type=jnp.float32
    )
    query_shift_grad = jnp.sum(query_grad, axis=(0, 1), dtype=jnp.float32)
    value_shift_grad = jnp.sum(value_grad, axis=(0, 1), dtype=jnp.float32)
    normed_terms = (
        jnp.einsum(
            "csh,dh->csd", query_grad, saved["query_full"], preferred_element_type=jnp.float32
        )
        + jnp.einsum("csh,dh->csd", key_grad, saved["key_full"], preferred_element_type=jnp.float32)
        + jnp.einsum(
            "csh,dh->csd", value_grad, saved["value_full"], preferred_element_type=jnp.float32
        )
    )
    normed_grad = lax.psum_scatter(
        normed_terms.astype(jnp.bfloat16), "tensor", scatter_dimension=1, tiled=True
    ).astype(jnp.float32)
    first_pull = jax.vjp(layer_norm, saved["rows"], saved["gain_one"], saved["bias_one"])[1]
    tokens_part, gain_one_grad, bias_one_grad = first_pull(normed_grad)
    tokens_grad = middle_grad + tokens_part
    summed = lax.psum(
        (
            gain_one_grad,
            bias_one_grad,
            out_shift_grad,
            gain_two_grad,
            bias_two_grad,
            down_shift_grad,
        ),
        "tensor",
    )
    owned = (
        lax.psum_scatter(
            query_weight_grad.astype(jnp.bfloat16), "dp", scatter_dimension=0, tiled=True
        ).astype(jnp.float32),
        lax.psum_scatter(
            key_weight_grad.astype(jnp.bfloat16), "dp", scatter_dimension=0, tiled=True
        ).astype(jnp.float32),
        lax.psum_scatter(
            value_weight_grad.astype(jnp.bfloat16), "dp", scatter_dimension=0, tiled=True
        ).astype(jnp.float32),
        lax.psum_scatter(
            out_grad.astype(jnp.bfloat16), "dp", scatter_dimension=0, tiled=True
        ).astype(jnp.float32),
        lax.psum_scatter(
            summed[0].astype(jnp.bfloat16), "dp", scatter_dimension=0, tiled=True
        ).astype(jnp.float32),
        lax.psum_scatter(
            summed[1].astype(jnp.bfloat16), "dp", scatter_dimension=0, tiled=True
        ).astype(jnp.float32),
        lax.psum_scatter(
            summed[2].astype(jnp.bfloat16), "dp", scatter_dimension=0, tiled=True
        ).astype(jnp.float32),
        lax.psum_scatter(
            summed[3].astype(jnp.bfloat16), "dp", scatter_dimension=0, tiled=True
        ).astype(jnp.float32),
        lax.psum_scatter(
            summed[4].astype(jnp.bfloat16), "dp", scatter_dimension=0, tiled=True
        ).astype(jnp.float32),
        lax.psum_scatter(
            summed[5].astype(jnp.bfloat16), "dp", scatter_dimension=0, tiled=True
        ).astype(jnp.float32),
    )
    shared = lax.psum((query_shift_grad, value_shift_grad, up_shift_grad), "dp")
    return (
        saved["output"].astype(jnp.bfloat16),
        tokens_grad,
        owned[4],
        owned[5],
        owned[0],
        shared[0],
        owned[1],
        owned[2],
        shared[1],
        owned[3],
        owned[6],
        owned[7],
        owned[8],
        up_grad_shard,
        shared[2],
        down_grad_shard,
        owned[9],
    )


def plane_local(
    tokens,
    lengths,
    cotangent,
    ln1_gain,
    ln1_bias,
    query_weight,
    query_bias,
    key_weight,
    value_weight,
    value_bias,
    out_weight,
    out_bias,
    ln2_gain,
    ln2_bias,
    up_weight,
    up_bias,
    down_weight,
    down_bias,
):
    planes = lax.axis_size("tensor")
    mine = lax.axis_index("dp")
    core, seat = mine & 1, mine >> 1
    plane = lax.axis_index("tensor")
    quarter, width = tokens.shape[1], tokens.shape[2]
    rows_of = query_weight.shape[0]
    sub = quarter // SEATS
    wide = query_weight.shape[1]
    heads = wide // HEAD_DIM
    hidden_of = up_weight.shape[1] // SEATS

    def at(stack, index):
        return lax.dynamic_index_in_dim(stack, index, 0, keepdims=False)

    vectors = (ln1_gain, ln1_bias, out_bias, ln2_gain, ln2_bias, down_bias)
    small = jnp.concatenate(
        [v.astype(jnp.float32) for v in vectors] + [lengths.astype(jnp.float32)]
    )
    small = lax.all_gather(small, "dp", axis=0)
    gain_one, bias_one, out_shift, gain_two, bias_two, down_shift = (
        small[:, k * rows_of : (k + 1) * rows_of].reshape(-1) for k in range(len(vectors))
    )
    length = at(small, 2 * plane + core)[-1].astype(jnp.int32)

    rows_low = to_plane(tokens[0], seat, plane, planes)
    cot_low = to_plane(cotangent[0], seat, plane, planes)

    def by_seat(w):
        return w.reshape(rows_of, SEATS, -1)

    pad = jnp.zeros((rows_of, SEATS, SLOT - 3 * HEAD_DIM), jnp.bfloat16)
    qkv_piece = jnp.concatenate(
        [by_seat(query_weight), by_seat(key_weight), by_seat(value_weight), pad], axis=2
    ).transpose(1, 0, 2)
    q_shift = at(query_bias.reshape(SEATS, HEAD_DIM), seat)
    v_shift = at(value_bias.reshape(SEATS, HEAD_DIM), seat)
    none = jnp.zeros((HEAD_DIM,), jnp.bfloat16)
    qkv_row = jnp.concatenate(
        [q_shift, none, v_shift, jnp.zeros((SLOT - 3 * HEAD_DIM,), jnp.bfloat16)]
    )
    qkv_blocks = line_gather(
        with_row(seat_exchange(qkv_piece, seat), qkv_row), planes, plane
    )
    qkv_half = jnp.concatenate([b[: SEATS * rows_of] for b in qkv_blocks], axis=1)
    qkv_full = both_cores(qkv_half, core, rows_of)
    qkv_shift = jnp.concatenate([b[SEATS * rows_of] for b in qkv_blocks])

    out_blocks = line_gather(out_weight, planes, plane)
    out_rows = (
        jnp.stack([b.reshape(rows_of, SEATS, HEAD_DIM) for b in out_blocks], axis=2)
    ).reshape(rows_of, SEATS * planes * HEAD_DIM)
    out_around = plane_gather(out_rows).reshape(SEATS, rows_of, -1)
    out_half = jnp.concatenate([at(out_around, s ^ seat) for s in range(SEATS)])
    out_full = both_cores(out_half, core, rows_of)

    ff_piece = jnp.concatenate([by_seat(up_weight), by_seat(down_weight)], axis=2).transpose(
        1, 0, 2
    )
    up_row = at(up_bias.reshape(SEATS, hidden_of), seat)
    ff_row = jnp.concatenate([up_row, jnp.zeros((hidden_of,), jnp.bfloat16)])
    ff_blocks = line_gather(with_row(seat_exchange(ff_piece, seat), ff_row), planes, plane)
    up_half = jnp.concatenate([b[: SEATS * rows_of, :hidden_of] for b in ff_blocks], axis=1)
    down_half = jnp.concatenate([b[: SEATS * rows_of, hidden_of:] for b in ff_blocks], axis=1)
    up_full = both_cores(up_half, core, rows_of)
    down_full = both_cores(down_half, core, rows_of)
    up_shift = jnp.concatenate([b[SEATS * rows_of, :hidden_of] for b in ff_blocks])

    rows = rows_low.astype(jnp.float32)
    normed = layer_norm(rows, gain_one, bias_one).astype(jnp.bfloat16)
    normed_all = plane_gather(normed)
    seq = normed_all.shape[0]
    qkv = (
        dot(normed_all, qkv_full, (1, 0)) + qkv_shift.astype(jnp.float32)
    ).astype(jnp.bfloat16)
    block, part, place = (
        lax.broadcasted_iota(jnp.int32, (SEATS, planes, sub), a) for a in range(3)
    )
    position = ((plane ^ part) * quarter + (seat ^ block) * sub + place).reshape(seq)
    valid = position < length
    shaped = qkv.reshape(seq, heads, SLOT)
    queries = shaped[:, :, :HEAD_DIM]
    keyed = shaped[:, :, HEAD_DIM : 2 * HEAD_DIM]
    valued = shaped[:, :, 2 * HEAD_DIM : 3 * HEAD_DIM]
    blocks = 2
    context, log_total = attend_clip(queries, keyed, valued, valid, blocks)
    context = context.reshape(SEATS, quarter, wide)
    context_from = jnp.stack(
        [context[0]] + [swap(context[r], r << 1) for r in range(1, SEATS)]
    )
    context_own = jnp.concatenate([at(context_from, s ^ seat) for s in range(SEATS)], axis=1)
    attended = dot(context_own, out_full, (1, 1))
    middle = rows + attended + out_shift
    normed_two = layer_norm(middle, gain_two, bias_two).astype(jnp.bfloat16)
    normed_two_all = plane_gather(normed_two)
    hidden_pre = dot(normed_two_all, up_full, (1, 0)) + up_shift.astype(jnp.float32)
    cot_all = plane_gather(cot_low)
    hidden_grad = dot(cot_all, down_full, (1, 0))
    normal = 0.5 * (1.0 + lax.erf(hidden_pre * (0.5**0.5)))
    slope = normal + hidden_pre * (jnp.exp(-0.5 * hidden_pre * hidden_pre) * (0.5 / jnp.pi) ** 0.5)
    hidden = (hidden_pre * normal).astype(jnp.bfloat16)
    pre_grad = (hidden_grad * slope).astype(jnp.bfloat16)

    normed_two_terms = dot(pre_grad, up_full, (1, 1))
    normed_two_grad = plane_scatter(normed_two_terms)
    mixed = plane_scatter(dot(hidden, down_full, (1, 1)))
    output = (middle + mixed + down_shift).astype(jnp.bfloat16)
    output_home = from_plane(output, seat, plane, planes)
    up_grad = dot(normed_two_all, pre_grad, (0, 0)).astype(jnp.bfloat16)
    down_grad = dot(cot_all, hidden, (0, 0)).astype(jnp.bfloat16)
    up_shift_grad = jnp.sum(pre_grad, axis=0, dtype=jnp.float32)
    grad_out = cot_low.astype(jnp.float32)
    down_shift_grad = jnp.sum(grad_out, axis=0)
    middle_part, gain_two_grad, bias_two_grad = norm_back(middle, gain_two, normed_two_grad)
    middle_grad = grad_out + middle_part
    out_shift_grad = jnp.sum(middle_grad, axis=0)
    middle_low = middle_grad.astype(jnp.bfloat16)

    context_grad_own = (
        dot(middle_low, out_full, (1, 0)).astype(jnp.bfloat16).reshape(quarter, SEATS, wide)
    ).transpose(1, 0, 2)
    context_grad = jnp.concatenate(
        [at(context_grad_own, seat)]
        + [swap(at(context_grad_own, seat ^ r), r << 1) for r in range(1, SEATS)]
    ).reshape(seq, heads, HEAD_DIM)
    out_grad = dot(middle_low, context_own, (0, 0)).astype(jnp.bfloat16)
    query_grad, key_grad, value_grad = attend_back(
        queries, keyed, valued, context_grad, log_total, valid, blocks
    )
    qkv_grad = jnp.concatenate(
        [
            query_grad,
            key_grad,
            value_grad,
            jnp.zeros((seq, heads, SLOT - 3 * HEAD_DIM), jnp.bfloat16),
        ],
        axis=2,
    ).reshape(seq, heads * SLOT)
    normed_grad = plane_scatter(dot(qkv_grad, qkv_full, (1, 1)))
    qkv_weight_grad = dot(normed_all, qkv_grad, (0, 0)).astype(jnp.bfloat16)
    qkv_shift_grad = jnp.sum(qkv_grad, axis=0, dtype=jnp.float32).reshape(planes, SLOT)
    tokens_part, gain_one_grad, bias_one_grad = norm_back(rows, gain_one, normed_grad)
    tokens_grad = (middle_grad + tokens_part).astype(jnp.bfloat16)
    tokens_grad_home = from_plane(tokens_grad, seat, plane, planes)

    def lanes(full, t, size):
        return full[..., t * size : (t + 1) * size]

    ff_grad = [
        jnp.concatenate([lanes(up_grad, t, hidden_of), lanes(down_grad, t, hidden_of)], axis=1)
        for t in range(planes)
    ]
    ff_home = weights_home(ff_grad, core, seat, rows_of, planes)
    up_home = jnp.concatenate([at(ff_home, s ^ seat)[:, :hidden_of] for s in range(SEATS)], axis=1)
    down_home = jnp.concatenate(
        [at(ff_home, s ^ seat)[:, hidden_of:] for s in range(SEATS)], axis=1
    )
    qkv_home = weights_home(
        [lanes(qkv_weight_grad, t, SLOT) for t in range(planes)], core, seat, rows_of, planes
    )
    query_home, key_home, value_home = (
        jnp.concatenate(
            [at(qkv_home, s ^ seat)[:, k * HEAD_DIM : (k + 1) * HEAD_DIM] for s in range(SEATS)],
            axis=1,
        )
        for k in range(3)
    )
    out_kept = core_scatter(out_grad, core, rows_of).astype(jnp.bfloat16)
    out_owned = plane_scatter(
        jnp.concatenate([at(out_kept, seat ^ r) for r in range(SEATS)])
    ).astype(jnp.bfloat16)
    out_owned = out_owned.reshape(rows_of, SEATS, planes, HEAD_DIM)
    out_home = line_scatter(
        [out_owned[:, :, t].reshape(rows_of, wide) for t in range(planes)], planes
    )

    def by_block(v):
        placed = jnp.stack([at(v, (plane - p) % planes) for p in range(planes)])
        seats = lax.broadcasted_iota(jnp.int32, (1, SEATS, 1), 1)
        return jnp.where(seats == seat, placed[:, None, :], 0.0).reshape(-1)

    def everywhere(v):
        for bit in (1, 2, 4):
            v = v + swap(v, bit)
        for bit in (1, 2):
            v = v + plane_swap(v, bit, planes)
        return v

    early = everywhere(
        jnp.concatenate(
            [gain_two_grad, bias_two_grad, out_shift_grad, down_shift_grad]
            + [by_block(up_shift_grad.reshape(planes, hidden_of))]
        )
    )
    late = everywhere(
        jnp.concatenate(
            [gain_one_grad, bias_one_grad]
            + [by_block(qkv_shift_grad[:, :HEAD_DIM])]
            + [by_block(qkv_shift_grad[:, 2 * HEAD_DIM : 3 * HEAD_DIM])]
        )
    )

    def owned(v, k, size, index):
        return lax.dynamic_slice_in_dim(v[k * width :], index * size, size)

    return (
        output_home[None],
        tokens_grad_home[None].astype(jnp.float32),
        owned(late, 0, rows_of, mine),
        owned(late, 1, rows_of, mine),
        query_home.astype(jnp.float32),
        owned(late, 2, wide, plane),
        key_home.astype(jnp.float32),
        value_home.astype(jnp.float32),
        owned(late, 3, wide, plane),
        out_home,
        owned(early, 2, rows_of, mine),
        owned(early, 0, rows_of, mine),
        owned(early, 1, rows_of, mine),
        up_home.astype(jnp.float32),
        owned(early, 4, SEATS * hidden_of, plane),
        down_home.astype(jnp.float32),
        owned(early, 3, rows_of, mine),
    )


def solution(mesh):
    one_plane = mesh.shape["dp"] == 2 * SEATS and mesh.shape["tensor"] == SEATS
    placed = (
        P("dp", "tensor", None),
        P("dp"),
        P("dp", "tensor", None),
        P("dp"),
        P("dp"),
        P("dp", "tensor"),
        P("tensor"),
        P("dp", "tensor"),
        P("dp", "tensor"),
        P("tensor"),
        P("dp", "tensor"),
        P("dp"),
        P("dp"),
        P("dp"),
        P("dp", "tensor"),
        P("tensor"),
        P("dp", "tensor"),
        P("dp"),
    )
    return jax.shard_map(
        plane_local if one_plane else local,
        mesh=mesh,
        in_specs=placed,
        out_specs=(
            P("dp", "tensor", None),
            P("dp", "tensor", None),
            P("dp"),
            P("dp"),
            P("dp", "tensor"),
            P("tensor"),
            P("dp", "tensor"),
            P("dp", "tensor"),
            P("tensor"),
            P("dp", "tensor"),
            P("dp"),
            P("dp"),
            P("dp"),
            P("dp", "tensor"),
            P("tensor"),
            P("dp", "tensor"),
            P("dp"),
        ),
        check_vma=False,
    )
```

```python
import jax
import jax.numpy as jnp
from jax import lax
from jax.experimental import pallas as pl
from jax.experimental.pallas import tpu as pltpu
from jax.sharding import Mesh
from jax.sharding import PartitionSpec as P

HEAD_DIM = 80


masked_score = -1e30


def layer_norm(values, gain, shift):
    centre = values - jnp.mean(values, axis=-1, keepdims=True)
    spread = jnp.mean(centre * centre, axis=-1, keepdims=True)
    return centre * lax.rsqrt(spread + 1e-05) * gain + shift


SEATS = 4
SLOT = 256
EXTRA = 16
MEGA = 1 << 20
LOG2E = 1.4426950408889634
CORES = ((0, 1), (1, 0))


def dot(left, right, dims):
    return lax.dot_general(
        left, right, (((dims[0],), (dims[1],)), ((), ())), preferred_element_type=jnp.float32
    )


def seat_swap(values, bits):
    return lax.ppermute(values, "seat", [(k, k ^ bits) for k in range(SEATS)])


def core_swap(values):
    return lax.ppermute(values, "core", CORES)


def plane_swap(values, bits, planes):
    return lax.ppermute(values, "tensor", [(k, k ^ bits) for k in range(planes)])


def at_index(stack, index):
    return lax.dynamic_index_in_dim(stack, index, 0, keepdims=False)


def to_plane(rows, seat, plane, planes):
    parts = rows.reshape(SEATS, -1, rows.shape[1])
    got = jnp.stack(
        [at_index(parts, seat)] + [seat_swap(at_index(parts, seat ^ r), r) for r in range(1, SEATS)]
    )
    turn = seat ^ plane
    return jnp.concatenate(
        [at_index(got, turn)]
        + [plane_swap(at_index(got, turn ^ k), k, planes) for k in range(1, planes)]
    )


def from_plane(rows, seat, plane, planes):
    parts = rows.reshape(planes, -1, rows.shape[1])
    got = jnp.stack([parts[0]] + [plane_swap(parts[k], k, planes) for k in range(1, planes)])
    turn = seat ^ plane
    back = jnp.stack(
        [at_index(got, turn)] + [seat_swap(at_index(got, turn ^ r), r) for r in range(1, SEATS)]
    )
    return jnp.concatenate([at_index(back, s ^ seat) for s in range(SEATS)])


def plane_gather(own):
    half = own.shape[0] // 2
    across, along = seat_swap(own, 1), seat_swap(own, 2)
    far_a, far_b = seat_swap(across[:half], 2), seat_swap(along[half:], 1)
    return jnp.concatenate([own, across, along, far_a, far_b])


def plane_scatter(terms):
    rows = terms.shape[0] // SEATS
    half = rows // 2
    own, across, along, far = (terms[k * rows : (k + 1) * rows] for k in range(SEATS))
    far = far.astype(jnp.bfloat16)
    far_a, far_b = seat_swap(far[:half], 1), seat_swap(far[half:], 2)
    along = jnp.concatenate([along[:half] + far_a.astype(jnp.float32), along[half:]])
    across = jnp.concatenate([across[:half], across[half:] + far_b.astype(jnp.float32)])
    along = seat_swap(along.astype(jnp.bfloat16), 2).astype(jnp.float32)
    across = seat_swap(across.astype(jnp.bfloat16), 1).astype(jnp.float32)
    return own + across + along


def smem():
    return pl.BlockSpec(memory_space=pltpu.SMEM)


def vmem():
    return pl.BlockSpec(memory_space=pltpu.VMEM)


def pack_weights(plan, columns, sources, extra, seat):
    rows = sources[0].shape[0]

    def kernel(seat_ref, *refs):
        inputs, extra_ref = refs[: len(sources)], refs[len(sources)]
        outs, held = refs[len(sources) + 1 : -1], refs[-1]
        used = max(lane + size for _, lane, size in plan)
        for j in range(SEATS):
            for k, lane, size in plan:
                held[j, :rows, lane : lane + size] = inputs[k][:, j * size : (j + 1) * size]
            if used < columns:
                held[j, :rows, used:] = jnp.zeros((rows, columns - used), jnp.bfloat16)
            held[j, rows:, :] = extra_ref[j]
        for r in range(SEATS):
            outs[r][...] = held[seat_ref[0] ^ r]

    piece = jax.ShapeDtypeStruct((rows + EXTRA, columns), jnp.bfloat16)
    return pl.pallas_call(
        kernel,
        out_shape=[piece] * SEATS,
        in_specs=[smem()] + [vmem()] * (len(sources) + 1),
        out_specs=[vmem()] * SEATS,
        scratch_shapes=[pltpu.VMEM((SEATS, rows + EXTRA, columns), jnp.bfloat16)],
        compiler_params=pltpu.CompilerParams(vmem_limit_bytes=16 * MEGA),
        name="pack_weights",
    )(seat, *sources, extra)


def assemble_weights(plan, gathered, seat, planes):
    groups, _, tall, columns = gathered.shape
    rows = tall - EXTRA

    def kernel(seat_ref, in_ref, *outs):
        del seat_ref
        for c in range(2):
            for z in range(planes):
                for k, (lane, size) in enumerate(plan):
                    outs[k][c * rows : (c + 1) * rows, z * size : (z + 1) * size] = in_ref[
                        c * planes + z, 0, :rows, lane : lane + size
                    ]
        outs[-1][0] = in_ref[:, 0, rows:, :]

    return pl.pallas_call(
        kernel,
        out_shape=[
            jax.ShapeDtypeStruct((SEATS * 2 * rows, planes * size), jnp.bfloat16)
            for _, size in plan
        ]
        + [jax.ShapeDtypeStruct((SEATS, groups, EXTRA, columns), jnp.bfloat16)],
        grid_spec=pltpu.PrefetchScalarGridSpec(
            num_scalar_prefetch=1,
            grid=(SEATS,),
            in_specs=[
                pl.BlockSpec((groups, 1, tall, columns), lambda s, seat: (0, s ^ seat[0], 0, 0))
            ],
            out_specs=[
                pl.BlockSpec((2 * rows, planes * size), lambda s, seat: (s, 0)) for _, size in plan
            ]
            + [pl.BlockSpec((1, groups, EXTRA, columns), lambda s, seat: (s, 0, 0, 0))],
        ),
        compiler_params=pltpu.CompilerParams(vmem_limit_bytes=24 * MEGA),
        name="assemble_weights",
    )(seat, gathered)


def pack_grads(plan, columns, sources, vectors, shift, core, planes):
    rows = sources[0].shape[0] // (2 * SEATS)
    tall = rows + EXTRA

    def kernel(core_ref, *refs):
        inputs, vec_ref, shift_ref = refs[: len(sources)], refs[len(sources)], refs[-3]
        for out, c in ((refs[-2], core_ref[0]), (refs[-1], 1 - core_ref[0])):
            start = pl.multiple_of(c * rows, 16)
            tile = vec_ref[0, c]
            line = lax.broadcasted_iota(jnp.int32, tile.shape, 0)
            for z in range(planes):
                for k, stride, lane, size in plan:
                    out[z, 0, :rows, lane : lane + size] = inputs[k][
                        pl.ds(start, rows), z * stride : z * stride + size
                    ]
                out[z, 0, rows:, :] = jnp.where(line == 8, shift_ref[z], tile).astype(jnp.bfloat16)

    chunk = jax.ShapeDtypeStruct((planes, SEATS, tall, columns), jnp.bfloat16)
    block = pl.BlockSpec((planes, 1, tall, columns), lambda s: (0, s, 0, 0))
    return pl.pallas_call(
        kernel,
        out_shape=[chunk, chunk],
        grid=(SEATS,),
        in_specs=[smem()]
        + [pl.BlockSpec((2 * rows, a.shape[1]), lambda s: (s, 0)) for a in sources]
        + [
            pl.BlockSpec((1, 2, EXTRA, columns), lambda s: (s, 0, 0, 0)),
            pl.BlockSpec((planes, 1, columns), lambda s: (0, 0, 0)),
        ],
        out_specs=[block, block],
        compiler_params=pltpu.CompilerParams(vmem_limit_bytes=32 * MEGA),
        name="pack_grads",
    )(core, *sources, vectors, shift)


def finish_grads(plan, pieces, seat):
    tall, columns = pieces[0].shape
    rows = tall - EXTRA

    def kernel(seat_ref, *refs):
        outs, held = refs[SEATS:-1], refs[-1]
        for r in range(SEATS):
            held[seat_ref[0] ^ r] = refs[r][...]
        for j in range(SEATS):
            for k, (lane, size) in enumerate(plan):
                outs[k][:, j * size : (j + 1) * size] = held[j, :rows, lane : lane + size].astype(
                    jnp.float32
                )
            outs[-1][j] = held[j, rows:, :].astype(jnp.float32)

    return pl.pallas_call(
        kernel,
        out_shape=[jax.ShapeDtypeStruct((rows, SEATS * size), jnp.float32) for _, size in plan]
        + [jax.ShapeDtypeStruct((SEATS, EXTRA, columns), jnp.float32)],
        in_specs=[smem()] + [vmem()] * SEATS,
        out_specs=[vmem()] * (len(plan) + 1),
        scratch_shapes=[pltpu.VMEM((SEATS, tall, columns), jnp.bfloat16)],
        compiler_params=pltpu.CompilerParams(vmem_limit_bytes=24 * MEGA),
        name="finish_grads",
    )(seat, *pieces)


def key_shift(facts_ref, shape, planes, quarter):
    length, seat, plane = facts_ref[0], facts_ref[1], facts_ref[2]
    row = lax.broadcasted_iota(jnp.int32, shape, 0)
    sub = quarter // SEATS
    block, part, place = row // quarter, (row // sub) % planes, row % sub
    position = (plane ^ part) * quarter + (seat ^ block) * sub + place
    return jnp.where(position < length, 0.0, masked_score).astype(jnp.float32)


def attend(facts, qkv, planes, quarter):
    seq = qkv.shape[1]
    scale = HEAD_DIM ** (-0.5) * LOG2E

    def kernel(facts_ref, qkv_ref, all_ref, *refs):
        outs, log_ref, shift_ref = refs[: SEATS - 1], refs[-2], refs[-1]

        @pl.when(pl.program_id(0) == 0)
        def _():
            shift_ref[...] = key_shift(facts_ref, shift_ref.shape, planes, quarter)

        keys = jnp.transpose(qkv_ref[HEAD_DIM : 2 * HEAD_DIM, :])
        values = qkv_ref[2 * HEAD_DIM : 3 * HEAD_DIM, :]
        for r in range(SEATS):
            at = slice(r * quarter, (r + 1) * quarter)
            scores = dot(keys, qkv_ref[:HEAD_DIM, at], (1, 0)) * scale + shift_ref[...]
            top = jnp.max(scores, axis=0, keepdims=True)
            expo = jnp.exp2(scores - top)
            total = jnp.sum(expo, axis=0, keepdims=True)
            context = dot(values, expo.astype(jnp.bfloat16), (1, 0)) / total
            context = context.astype(jnp.bfloat16)
            all_ref[:, at] = context
            if r:
                outs[r - 1][...] = context
            log_ref[0, :, at] = top + jnp.log2(total)

    head = pl.BlockSpec((HEAD_DIM, quarter), lambda h: (h, 0))
    return pl.pallas_call(
        kernel,
        out_shape=[jax.ShapeDtypeStruct((planes * HEAD_DIM, seq), jnp.bfloat16)]
        + [jax.ShapeDtypeStruct((planes * HEAD_DIM, quarter), jnp.bfloat16)] * (SEATS - 1)
        + [jax.ShapeDtypeStruct((planes, 1, seq), jnp.float32)],
        grid=(planes,),
        in_specs=[smem(), pl.BlockSpec((SLOT, seq), lambda h: (h, 0))],
        out_specs=[pl.BlockSpec((HEAD_DIM, seq), lambda h: (h, 0))]
        + [head] * (SEATS - 1)
        + [pl.BlockSpec((1, 1, seq), lambda h: (h, 0, 0))],
        scratch_shapes=[pltpu.VMEM((seq, quarter), jnp.float32)],
        compiler_params=pltpu.CompilerParams(vmem_limit_bytes=40 * MEGA),
        name="attend",
    )(facts, qkv)


def attend_grad(facts, qkv, context_grad, logs, planes, quarter):
    seq = qkv.shape[1]
    scale = HEAD_DIM ** (-0.5)

    def kernel(facts_ref, qkv_ref, grad_ref, log_ref, out_ref, shift_ref, key_acc, value_acc):
        @pl.when(pl.program_id(0) == 0)
        def _():
            shift_ref[...] = key_shift(facts_ref, shift_ref.shape, planes, quarter)

        keys = jnp.transpose(qkv_ref[HEAD_DIM : 2 * HEAD_DIM, :])
        values = jnp.transpose(qkv_ref[2 * HEAD_DIM : 3 * HEAD_DIM, :])
        for r in range(SEATS):
            at = slice(r * quarter, (r + 1) * quarter)
            queries, grad = qkv_ref[:HEAD_DIM, at], grad_ref[:, at]
            scores = dot(keys, queries, (1, 0)) * (scale * LOG2E) + shift_ref[...]
            probs = jnp.exp2(scores - log_ref[0, :, at])
            prob_grad = dot(values, grad, (1, 0))
            mean = jnp.sum(probs * prob_grad, axis=0, keepdims=True)
            score_grad = (probs * (prob_grad - mean)).astype(jnp.bfloat16)
            query_grad = dot(qkv_ref[HEAD_DIM : 2 * HEAD_DIM, :], score_grad, (1, 0))
            out_ref[:HEAD_DIM, at] = (query_grad * scale).astype(jnp.bfloat16)
            key_part = dot(queries, score_grad, (1, 1))
            value_part = dot(grad, probs.astype(jnp.bfloat16), (1, 1))
            if r == 0:
                key_acc[...] = key_part
                value_acc[...] = value_part
            else:
                key_acc[...] += key_part
                value_acc[...] += value_part
        out_ref[HEAD_DIM : 2 * HEAD_DIM, :] = (key_acc[...] * scale).astype(jnp.bfloat16)
        out_ref[2 * HEAD_DIM : 3 * HEAD_DIM, :] = value_acc[...].astype(jnp.bfloat16)
        out_ref[3 * HEAD_DIM :, :] = jnp.zeros((SLOT - 3 * HEAD_DIM, seq), jnp.bfloat16)

    return pl.pallas_call(
        kernel,
        out_shape=jax.ShapeDtypeStruct((planes * SLOT, seq), jnp.bfloat16),
        grid=(planes,),
        in_specs=[
            smem(),
            pl.BlockSpec((SLOT, seq), lambda h: (h, 0)),
            pl.BlockSpec((HEAD_DIM, seq), lambda h: (h, 0)),
            pl.BlockSpec((1, 1, seq), lambda h: (h, 0, 0)),
        ],
        out_specs=pl.BlockSpec((SLOT, seq), lambda h: (h, 0)),
        scratch_shapes=[
            pltpu.VMEM((seq, quarter), jnp.float32),
            pltpu.VMEM((HEAD_DIM, seq), jnp.float32),
            pltpu.VMEM((HEAD_DIM, seq), jnp.float32),
        ],
        compiler_params=pltpu.CompilerParams(vmem_limit_bytes=48 * MEGA),
        name="attend_grad",
    )(facts, qkv, context_grad, logs)


def norm_back(values, gain, grad):
    mean = jnp.mean(values, axis=-1, keepdims=True)
    centre = values - mean
    root = lax.rsqrt(jnp.mean(centre * centre, axis=-1, keepdims=True) + 1e-05)
    unit = centre * root
    scaled = grad * gain
    part = root * (
        scaled
        - jnp.mean(scaled, axis=-1, keepdims=True)
        - unit * jnp.mean(scaled * unit, axis=-1, keepdims=True)
    )
    return part, jnp.sum(grad * unit, axis=0), jnp.sum(grad, axis=0)


def weights_home(kept, given, seat):
    both = (kept.astype(jnp.float32) + core_swap(given).astype(jnp.float32)).astype(jnp.bfloat16)
    owned = lax.psum_scatter(both, "tensor", scatter_dimension=0, tiled=False)
    return [at_index(owned, seat)] + [
        seat_swap(at_index(owned, seat ^ r), r) for r in range(1, SEATS)
    ]


def masked_scores(query_part, key_rows, valid, scale):
    scores = (
        jnp.einsum("qhe,khe->hqk", query_part, key_rows, preferred_element_type=jnp.float32) * scale
    )
    return jnp.where(valid[None, None, :], scores, masked_score)


def attend_clip(query_rows, key_rows, value_rows, valid, blocks):
    seq, heads = (query_rows.shape[0], query_rows.shape[1])
    scale = HEAD_DIM ** (-0.5)
    query_blocks = query_rows.reshape(blocks, seq // blocks, heads, HEAD_DIM)

    def one_block(query_part):
        scores = masked_scores(query_part, key_rows, valid, scale)
        top = jnp.max(scores, axis=-1, keepdims=True)
        expo = jnp.exp(scores - top)
        total = jnp.sum(expo, axis=-1, keepdims=True)
        probs = (expo / total).astype(jnp.bfloat16)
        context = jnp.einsum(
            "hqk,khe->qhe", probs, value_rows, preferred_element_type=jnp.float32
        ).astype(jnp.bfloat16)
        return (context, (top + jnp.log(total))[..., 0])

    context, log_total = lax.map(one_block, query_blocks)
    return (context.reshape(seq, heads, HEAD_DIM), log_total)


def attend_back(query_rows, key_rows, value_rows, context_grad, log_total, valid, blocks):
    seq, heads = (query_rows.shape[0], query_rows.shape[1])
    scale = HEAD_DIM ** (-0.5)
    query_blocks = query_rows.reshape(blocks, seq // blocks, heads, HEAD_DIM)
    grad_blocks = context_grad.reshape(blocks, seq // blocks, heads, HEAD_DIM)

    def one_block(carry, inputs):
        key_acc, value_acc = carry
        query_part, grad_part, lse_part = inputs
        scores = masked_scores(query_part, key_rows, valid, scale)
        probs = jnp.exp(scores - lse_part[..., None])
        value_acc = value_acc + jnp.einsum(
            "hqk,qhe->khe",
            probs.astype(jnp.bfloat16),
            grad_part,
            preferred_element_type=jnp.float32,
        )
        prob_grad = jnp.einsum(
            "qhe,khe->hqk", grad_part, value_rows, preferred_element_type=jnp.float32
        )
        centred = prob_grad - jnp.sum(probs * prob_grad, axis=-1, keepdims=True)
        score_grad = (probs * centred).astype(jnp.bfloat16)
        query_grad = (
            jnp.einsum("hqk,khe->qhe", score_grad, key_rows, preferred_element_type=jnp.float32)
            * scale
        )
        key_acc = (
            key_acc
            + jnp.einsum("hqk,qhe->khe", score_grad, query_part, preferred_element_type=jnp.float32)
            * scale
        )
        return ((key_acc, value_acc), query_grad.astype(jnp.bfloat16))

    zeros = jnp.zeros((seq, heads, HEAD_DIM), jnp.float32)
    (key_acc, value_acc), query_grad = lax.scan(
        one_block, (zeros, zeros), (query_blocks, grad_blocks, log_total)
    )
    return (
        query_grad.reshape(seq, heads, HEAD_DIM),
        key_acc.astype(jnp.bfloat16),
        value_acc.astype(jnp.bfloat16),
    )


def forward_pass(tokens, lengths, weights):
    (
        ln1_gain,
        ln1_bias,
        query_weight,
        query_bias,
        key_weight,
        value_weight,
        value_bias,
        out_weight,
        out_bias,
        ln2_gain,
        ln2_bias,
        up_weight,
        up_bias,
        down_weight,
        down_bias,
    ) = weights
    query_full, key_full, value_full, out_full, gain_one, bias_one, out_shift = (
        lax.all_gather(query_weight, "dp", axis=0, tiled=True),
        lax.all_gather(key_weight, "dp", axis=0, tiled=True),
        lax.all_gather(value_weight, "dp", axis=0, tiled=True),
        lax.all_gather(out_weight, "dp", axis=0, tiled=True),
        lax.all_gather(ln1_gain, "dp", axis=0, tiled=True),
        lax.all_gather(ln1_bias, "dp", axis=0, tiled=True),
        lax.all_gather(out_bias, "dp", axis=0, tiled=True),
    )
    gain_one = gain_one.astype(jnp.float32)
    bias_one = bias_one.astype(jnp.float32)
    rows = tokens.astype(jnp.float32)
    normed = layer_norm(rows, gain_one, bias_one).astype(jnp.bfloat16)
    normed_all = lax.all_gather(normed, "tensor", axis=1, tiled=True)
    clips, seq = (normed_all.shape[0], normed_all.shape[1])
    heads = query_full.shape[1] // HEAD_DIM
    blocks = seq // 512
    shaped = (clips, seq, heads, HEAD_DIM)
    queries = (
        (
            jnp.einsum("csd,dh->csh", normed_all, query_full, preferred_element_type=jnp.float32)
            + query_bias.astype(jnp.float32)
        )
        .astype(jnp.bfloat16)
        .reshape(shaped)
    )
    keyed = (
        jnp.einsum("csd,dh->csh", normed_all, key_full, preferred_element_type=jnp.float32)
        .astype(jnp.bfloat16)
        .reshape(shaped)
    )
    valued = (
        (
            jnp.einsum("csd,dh->csh", normed_all, value_full, preferred_element_type=jnp.float32)
            + value_bias.astype(jnp.float32)
        )
        .astype(jnp.bfloat16)
        .reshape(shaped)
    )

    def clip_attend(item):
        valid = lax.broadcasted_iota(jnp.int32, (seq,), 0) < item[3]
        return attend_clip(item[0], item[1], item[2], valid, blocks)

    context, log_total = lax.map(clip_attend, (queries, keyed, valued, lengths))
    context = context.reshape(clips, seq, heads * HEAD_DIM)
    attn_terms = jnp.einsum("csh,dh->csd", context, out_full, preferred_element_type=jnp.float32)
    attended = lax.psum_scatter(
        attn_terms.astype(jnp.bfloat16), "tensor", scatter_dimension=1, tiled=True
    ).astype(jnp.float32)
    middle = rows + attended + out_shift.astype(jnp.float32)
    up_full, down_full, gain_two, bias_two, down_shift = (
        lax.all_gather(up_weight, "dp", axis=0, tiled=True),
        lax.all_gather(down_weight, "dp", axis=0, tiled=True),
        lax.all_gather(ln2_gain, "dp", axis=0, tiled=True),
        lax.all_gather(ln2_bias, "dp", axis=0, tiled=True),
        lax.all_gather(down_bias, "dp", axis=0, tiled=True),
    )
    gain_two = gain_two.astype(jnp.float32)
    bias_two = bias_two.astype(jnp.float32)
    normed_two = layer_norm(middle, gain_two, bias_two).astype(jnp.bfloat16)
    normed_two_all = lax.all_gather(normed_two, "tensor", axis=1, tiled=True)
    hidden_pre = jnp.einsum(
        "csd,df->csf", normed_two_all, up_full, preferred_element_type=jnp.float32
    ) + up_bias.astype(jnp.float32)
    hidden = jax.nn.gelu(hidden_pre, approximate=False).astype(jnp.bfloat16)
    mlp_terms = jnp.einsum("csf,df->csd", hidden, down_full, preferred_element_type=jnp.float32)
    mixed = lax.psum_scatter(
        mlp_terms.astype(jnp.bfloat16), "tensor", scatter_dimension=1, tiled=True
    ).astype(jnp.float32)
    output = middle + mixed + down_shift.astype(jnp.float32)
    return {
        "output": output,
        "rows": rows,
        "normed_all": normed_all,
        "queries": queries,
        "keyed": keyed,
        "valued": valued,
        "context": context,
        "log_total": log_total,
        "middle": middle,
        "normed_two_all": normed_two_all,
        "hidden_pre": hidden_pre,
        "hidden": hidden,
        "query_full": query_full,
        "key_full": key_full,
        "value_full": value_full,
        "out_full": out_full,
        "up_full": up_full,
        "down_full": down_full,
        "gain_one": gain_one,
        "bias_one": bias_one,
        "gain_two": gain_two,
        "bias_two": bias_two,
        "blocks": blocks,
    }


def local(
    tokens,
    lengths,
    cotangent,
    ln1_gain,
    ln1_bias,
    query_weight,
    query_bias,
    key_weight,
    value_weight,
    value_bias,
    out_weight,
    out_bias,
    ln2_gain,
    ln2_bias,
    up_weight,
    up_bias,
    down_weight,
    down_bias,
):
    weights = (
        ln1_gain,
        ln1_bias,
        query_weight,
        query_bias,
        key_weight,
        value_weight,
        value_bias,
        out_weight,
        out_bias,
        ln2_gain,
        ln2_bias,
        up_weight,
        up_bias,
        down_weight,
        down_bias,
    )
    saved = forward_pass(tokens, lengths, weights)
    blocks = saved["blocks"]
    grad_out = cotangent.astype(jnp.float32)
    down_shift_grad = jnp.sum(grad_out, axis=(0, 1))
    grad_out_all = lax.all_gather(cotangent, "tensor", axis=1, tiled=True)
    down_grad = jnp.einsum(
        "csd,csf->df", grad_out_all, saved["hidden"], preferred_element_type=jnp.float32
    )
    hidden_grad = jnp.einsum(
        "csd,df->csf", grad_out_all, saved["down_full"], preferred_element_type=jnp.float32
    )
    gelu_pull = jax.vjp(lambda pre: jax.nn.gelu(pre, approximate=False), saved["hidden_pre"])[1]
    pre_grad = gelu_pull(hidden_grad)[0].astype(jnp.bfloat16)
    up_shift_grad = jnp.sum(pre_grad, axis=(0, 1), dtype=jnp.float32)
    up_grad = jnp.einsum(
        "csd,csf->df", saved["normed_two_all"], pre_grad, preferred_element_type=jnp.float32
    )
    up_grad_shard, down_grad_shard = (
        lax.psum_scatter(
            up_grad.astype(jnp.bfloat16), "dp", scatter_dimension=0, tiled=True
        ).astype(jnp.float32),
        lax.psum_scatter(
            down_grad.astype(jnp.bfloat16), "dp", scatter_dimension=0, tiled=True
        ).astype(jnp.float32),
    )
    normed_two_terms = jnp.einsum(
        "csf,df->csd", pre_grad, saved["up_full"], preferred_element_type=jnp.float32
    )
    normed_two_grad = lax.psum_scatter(
        normed_two_terms.astype(jnp.bfloat16), "tensor", scatter_dimension=1, tiled=True
    ).astype(jnp.float32)
    norm_pull = jax.vjp(layer_norm, saved["middle"], saved["gain_two"], saved["bias_two"])[1]
    middle_part, gain_two_grad, bias_two_grad = norm_pull(normed_two_grad)
    middle_grad = grad_out + middle_part
    out_shift_grad = jnp.sum(middle_grad, axis=(0, 1))
    middle_all = lax.all_gather(middle_grad.astype(jnp.bfloat16), "tensor", axis=1, tiled=True)
    out_grad = jnp.einsum(
        "csd,csh->dh", middle_all, saved["context"], preferred_element_type=jnp.float32
    )
    context_grad = jnp.einsum(
        "csd,dh->csh", middle_all, saved["out_full"], preferred_element_type=jnp.float32
    ).astype(jnp.bfloat16)
    queries = saved["queries"]
    clips, seq, heads = (queries.shape[0], queries.shape[1], queries.shape[2])

    def clip_back(item):
        valid = lax.broadcasted_iota(jnp.int32, (seq,), 0) < item[5]
        return attend_back(item[0], item[1], item[2], item[3], item[4], valid, blocks)

    query_grad, key_grad, value_grad = lax.map(
        clip_back,
        (
            queries,
            saved["keyed"],
            saved["valued"],
            context_grad.reshape(clips, seq, heads, HEAD_DIM),
            saved["log_total"],
            lengths,
        ),
    )
    flat = (clips, seq, heads * HEAD_DIM)
    query_grad = query_grad.reshape(flat)
    key_grad = key_grad.reshape(flat)
    value_grad = value_grad.reshape(flat)
    normed_all = saved["normed_all"]
    query_weight_grad = jnp.einsum(
        "csd,csh->dh", normed_all, query_grad, preferred_element_type=jnp.float32
    )
    key_weight_grad = jnp.einsum(
        "csd,csh->dh", normed_all, key_grad, preferred_element_type=jnp.float32
    )
    value_weight_grad = jnp.einsum(
        "csd,csh->dh", normed_all, value_grad, preferred_element_type=jnp.float32
    )
    query_shift_grad = jnp.sum(query_grad, axis=(0, 1), dtype=jnp.float32)
    value_shift_grad = jnp.sum(value_grad, axis=(0, 1), dtype=jnp.float32)
    normed_terms = (
        jnp.einsum(
            "csh,dh->csd", query_grad, saved["query_full"], preferred_element_type=jnp.float32
        )
        + jnp.einsum("csh,dh->csd", key_grad, saved["key_full"], preferred_element_type=jnp.float32)
        + jnp.einsum(
            "csh,dh->csd", value_grad, saved["value_full"], preferred_element_type=jnp.float32
        )
    )
    normed_grad = lax.psum_scatter(
        normed_terms.astype(jnp.bfloat16), "tensor", scatter_dimension=1, tiled=True
    ).astype(jnp.float32)
    first_pull = jax.vjp(layer_norm, saved["rows"], saved["gain_one"], saved["bias_one"])[1]
    tokens_part, gain_one_grad, bias_one_grad = first_pull(normed_grad)
    tokens_grad = middle_grad + tokens_part
    summed = lax.psum(
        (
            gain_one_grad,
            bias_one_grad,
            out_shift_grad,
            gain_two_grad,
            bias_two_grad,
            down_shift_grad,
        ),
        "tensor",
    )
    owned = (
        lax.psum_scatter(
            query_weight_grad.astype(jnp.bfloat16), "dp", scatter_dimension=0, tiled=True
        ).astype(jnp.float32),
        lax.psum_scatter(
            key_weight_grad.astype(jnp.bfloat16), "dp", scatter_dimension=0, tiled=True
        ).astype(jnp.float32),
        lax.psum_scatter(
            value_weight_grad.astype(jnp.bfloat16), "dp", scatter_dimension=0, tiled=True
        ).astype(jnp.float32),
        lax.psum_scatter(
            out_grad.astype(jnp.bfloat16), "dp", scatter_dimension=0, tiled=True
        ).astype(jnp.float32),
        lax.psum_scatter(
            summed[0].astype(jnp.bfloat16), "dp", scatter_dimension=0, tiled=True
        ).astype(jnp.float32),
        lax.psum_scatter(
            summed[1].astype(jnp.bfloat16), "dp", scatter_dimension=0, tiled=True
        ).astype(jnp.float32),
        lax.psum_scatter(
            summed[2].astype(jnp.bfloat16), "dp", scatter_dimension=0, tiled=True
        ).astype(jnp.float32),
        lax.psum_scatter(
            summed[3].astype(jnp.bfloat16), "dp", scatter_dimension=0, tiled=True
        ).astype(jnp.float32),
        lax.psum_scatter(
            summed[4].astype(jnp.bfloat16), "dp", scatter_dimension=0, tiled=True
        ).astype(jnp.float32),
        lax.psum_scatter(
            summed[5].astype(jnp.bfloat16), "dp", scatter_dimension=0, tiled=True
        ).astype(jnp.float32),
    )
    shared = lax.psum((query_shift_grad, value_shift_grad, up_shift_grad), "dp")
    return (
        saved["output"].astype(jnp.bfloat16),
        tokens_grad,
        owned[4],
        owned[5],
        owned[0],
        shared[0],
        owned[1],
        owned[2],
        shared[1],
        owned[3],
        owned[6],
        owned[7],
        owned[8],
        up_grad_shard,
        shared[2],
        down_grad_shard,
        owned[9],
    )


def plane_local(
    tokens,
    lengths,
    cotangent,
    ln1_gain,
    ln1_bias,
    query_weight,
    query_bias,
    key_weight,
    value_weight,
    value_bias,
    out_weight,
    out_bias,
    ln2_gain,
    ln2_bias,
    up_weight,
    up_bias,
    down_weight,
    down_bias,
):
    planes = lax.axis_size("tensor")
    core, seat = lax.axis_index("core"), lax.axis_index("seat")
    plane = lax.axis_index("tensor")
    seat_word, core_word = seat.reshape(1), core.reshape(1)
    quarter, width = tokens.shape[1], tokens.shape[2]
    rows_of = query_weight.shape[0]
    wide = query_weight.shape[1]
    hidden_of = up_weight.shape[1] // SEATS
    low, full = jnp.bfloat16, jnp.float32
    group = ("core", "tensor")

    vectors = jnp.stack([ln1_gain, ln1_bias, out_bias, ln2_gain, ln2_bias, down_bias])
    sizes = jnp.stack([lengths // 8, lengths % 8], axis=1).astype(low)
    extra = jnp.concatenate(
        [
            jnp.pad(vectors, ((0, 0), (0, SLOT - rows_of))),
            jnp.pad(sizes, ((0, 0), (0, SLOT - 2))),
            jnp.zeros((EXTRA - 7, SLOT), low),
        ]
    )
    heads_shift = jnp.concatenate(
        [
            query_bias.reshape(SEATS, HEAD_DIM),
            jnp.zeros((SEATS, HEAD_DIM), low),
            value_bias.reshape(SEATS, HEAD_DIM),
            jnp.zeros((SEATS, SLOT - 3 * HEAD_DIM), low),
        ],
        axis=1,
    )
    line = lax.broadcasted_iota(jnp.int32, (1, EXTRA, 1), 1)
    extra = jnp.where(line == 8, heads_shift[:, None, :], extra[None])
    qkv_pieces = pack_weights(
        [(0, 0, HEAD_DIM), (1, HEAD_DIM, HEAD_DIM), (2, 2 * HEAD_DIM, HEAD_DIM)],
        SLOT,
        [query_weight, key_weight, value_weight],
        extra,
        seat_word,
    )
    qkv_pieces = [qkv_pieces[0]] + [seat_swap(qkv_pieces[r], r) for r in range(1, SEATS)]
    qkv_around = lax.all_gather(jnp.stack(qkv_pieces), group, axis=0)

    rows_low = to_plane(tokens[0], seat, plane, planes)
    tokens_all = plane_gather(rows_low)
    seq = tokens_all.shape[0]

    ff_extra = jnp.pad(
        up_bias.reshape(SEATS, 1, hidden_of), ((0, 0), (0, EXTRA - 1), (0, hidden_of))
    )
    ff_pieces = pack_weights(
        [(0, 0, hidden_of), (1, hidden_of, hidden_of)],
        2 * hidden_of,
        [up_weight, down_weight],
        ff_extra,
        seat_word,
    )
    ff_pieces = [ff_pieces[0]] + [seat_swap(ff_pieces[r], r) for r in range(1, SEATS)]
    ff_around = lax.all_gather(jnp.stack(ff_pieces), group, axis=0)
    out_around = lax.all_gather(out_weight, ("seat", "core", "tensor"), axis=0)
    out_full = (
        out_around.reshape(2 * SEATS, planes, rows_of, wide)
        .transpose(0, 2, 1, 3)
        .reshape(width, planes * wide)
    )
    out_part = lax.dynamic_index_in_dim(
        out_full.reshape(width, planes, SEATS, HEAD_DIM), seat, 2, keepdims=False
    ).reshape(width, planes * HEAD_DIM)

    qkv_full, qkv_extra = assemble_weights([(0, SLOT)], qkv_around, seat_word, planes)
    vectors = qkv_extra[:, ::planes, :6, :rows_of].astype(full)
    gain_one, bias_one, out_shift, gain_two, bias_two, down_shift = (
        vectors[:, :, k].reshape(width) for k in range(6)
    )
    qkv_shift = qkv_extra[0, :planes, 8].astype(full).reshape(planes * SLOT, 1)
    size = lax.dynamic_index_in_dim(at_index(qkv_extra, plane), core * planes, 0, keepdims=False)
    length = (8.0 * size[6, 0].astype(full) + size[6, 1].astype(full)).astype(jnp.int32)
    facts = jnp.stack([length, seat, plane])

    up_full, down_full, ff_extra = assemble_weights(
        [(0, hidden_of), (hidden_of, hidden_of)], ff_around, seat_word, planes
    )
    up_shift = ff_extra[0, :planes, 0, :hidden_of].astype(full).reshape(planes * hidden_of)

    cot_low = to_plane(cotangent[0], seat, plane, planes)
    cot_all = plane_gather(cot_low)

    rows = rows_low.astype(full)
    normed_all = layer_norm(tokens_all.astype(full), gain_one, bias_one).astype(low)
    qkv = (dot(qkv_full, normed_all, (0, 1)) + qkv_shift).astype(low)
    context, *context_parts, logs = attend(facts, qkv, planes, quarter)
    context_own = jnp.zeros((planes, SEATS, HEAD_DIM, quarter), low)
    for r in range(SEATS):
        part = seat_swap(context_parts[r - 1], r) if r else context[:, :quarter]
        context_own = lax.dynamic_update_index_in_dim(
            context_own, part.reshape(planes, HEAD_DIM, quarter), seat ^ r, 1
        )
    context_own = context_own.reshape(planes * wide, quarter)
    middle = rows + dot(context_own, out_full, (0, 1)) + out_shift
    normed_two = layer_norm(middle, gain_two, bias_two).astype(low)
    normed_two_all = plane_gather(normed_two)
    hidden_grad = dot(cot_all, down_full, (1, 0))
    hidden_pre = dot(normed_two_all, up_full, (1, 0)) + up_shift
    normal = 0.5 * (1.0 + lax.erf(hidden_pre * (0.5**0.5)))
    slope = normal + hidden_pre * (jnp.exp(-0.5 * hidden_pre * hidden_pre) * (0.5 / jnp.pi) ** 0.5)
    hidden = (hidden_pre * normal).astype(low)
    pre_grad = (hidden_grad * slope).astype(low)

    normed_two_grad = plane_scatter(dot(pre_grad, up_full, (1, 1)))
    mixed = plane_scatter(dot(hidden, down_full, (1, 1)))
    output = (middle + mixed + down_shift).astype(low)
    output_home = from_plane(output, seat, plane, planes)
    grad_out = cot_low.astype(full)
    middle_part, gain_two_grad, bias_two_grad = norm_back(middle, gain_two, normed_two_grad)
    middle_grad = grad_out + middle_part
    middle_low = middle_grad.astype(low)
    middle_all = plane_gather(middle_low)

    def by_owner(sums, columns):
        placed = jnp.stack(sums).reshape(len(sums), SEATS, 2, rows_of).transpose(1, 2, 0, 3)
        return jnp.pad(
            placed, ((0, 0), (0, 0), (0, EXTRA - len(sums)), (0, columns - rows_of))
        )

    up_grad = dot(normed_two_all, pre_grad, (0, 0)).astype(low)
    down_grad = dot(cot_all, hidden, (0, 0)).astype(low)
    up_shift_grad = jnp.sum(pre_grad, axis=0, dtype=full).reshape(planes, 1, hidden_of)
    ff_kept, ff_given = pack_grads(
        [(0, hidden_of, 0, hidden_of), (1, hidden_of, hidden_of, hidden_of)],
        2 * hidden_of,
        [up_grad, down_grad],
        by_owner(
            [gain_two_grad, bias_two_grad, jnp.sum(middle_grad, axis=0), jnp.sum(grad_out, axis=0)],
            2 * hidden_of,
        ),
        jnp.pad(up_shift_grad, ((0, 0), (0, 0), (0, hidden_of))),
        core_word,
        planes,
    )
    ff_home = weights_home(ff_kept, ff_given, seat)
    up_home, down_home, ff_rest = finish_grads(
        [(0, hidden_of), (hidden_of, hidden_of)], ff_home, seat_word
    )
    ff_sums = jnp.sum(ff_rest[:, :4, :rows_of], axis=0)
    up_shift_home = ff_rest[:, 8, :hidden_of].reshape(SEATS * hidden_of)

    context_grad = dot(out_part, middle_all, (0, 1)).astype(low)
    out_grad = dot(middle_all, context, (0, 1)).astype(low)
    qkv_grad = attend_grad(facts, qkv, context_grad, logs, planes, quarter)
    normed_grad = plane_scatter(dot(qkv_grad, qkv_full, (0, 1)))
    tokens_part, gain_one_grad, bias_one_grad = norm_back(rows, gain_one, normed_grad)
    tokens_grad = (middle_grad + tokens_part).astype(low)
    tokens_grad_home = from_plane(tokens_grad, seat, plane, planes)
    ones = jnp.concatenate([gain_one_grad, bias_one_grad])
    ones = ones + core_swap(ones)
    for bits in (1, 2):
        ones = ones + seat_swap(ones, bits)
    for bits in (1, 2):
        ones = ones + plane_swap(ones, bits, planes)
    ones = lax.dynamic_slice_in_dim(
        ones.reshape(2, width), (2 * seat + core) * rows_of, rows_of, 1
    )

    qkv_weight_grad = dot(normed_all, qkv_grad, (0, 1)).astype(low)
    qkv_shift_grad = jnp.sum(qkv_grad, axis=1, dtype=full).reshape(planes, 1, SLOT)
    columns = 4 * HEAD_DIM
    qkv_kept, qkv_given = pack_grads(
        [(0, SLOT, 0, 3 * HEAD_DIM), (1, HEAD_DIM, 3 * HEAD_DIM, HEAD_DIM)],
        columns,
        [qkv_weight_grad, out_grad],
        jnp.zeros((SEATS, 2, EXTRA, columns), full),
        jnp.pad(qkv_shift_grad, ((0, 0), (0, 0), (0, columns - SLOT))),
        core_word,
        planes,
    )
    qkv_home = weights_home(qkv_kept, qkv_given, seat)
    query_home, key_home, value_home, out_home, qkv_rest = finish_grads(
        [(k * HEAD_DIM, HEAD_DIM) for k in range(4)], qkv_home, seat_word
    )
    query_shift_home = qkv_rest[:, 8, :HEAD_DIM].reshape(wide)
    value_shift_home = qkv_rest[:, 8, 2 * HEAD_DIM : 3 * HEAD_DIM].reshape(wide)

    return (
        output_home[None],
        tokens_grad_home[None].astype(full),
        ones[0],
        ones[1],
        query_home,
        query_shift_home,
        key_home,
        value_home,
        value_shift_home,
        out_home,
        ff_sums[2],
        ff_sums[0],
        ff_sums[1],
        up_home,
        up_shift_home,
        down_home,
        ff_sums[3],
    )


def specs(rows, columns):
    both = (P(rows, columns, None), P(rows), P(rows, columns), P(columns))
    cube, first, matrix, second = both
    ins = (cube, first, cube, first, first, matrix, second, matrix, matrix, second, matrix)
    ins += (first, first, first, matrix, second, matrix, first)
    outs = (cube, cube, first, first, matrix, second, matrix, matrix, second, matrix)
    outs += (first, first, first, matrix, second, matrix, first)
    return ins, outs


def solution(mesh):
    step, rows = local, "dp"
    if mesh.shape["dp"] == 2 * SEATS and mesh.shape["tensor"] == SEATS:
        devices = mesh.devices.reshape(SEATS, 2, SEATS)
        step, rows, mesh = plane_local, ("seat", "core"), Mesh(devices, ("seat", "core", "tensor"))
    ins, outs = specs(rows, "tensor")
    return jax.shard_map(step, mesh=mesh, in_specs=ins, out_specs=outs, check_vma=False)
```

```python
import jax
import jax.numpy as jnp
from jax import lax
from jax.experimental import pallas as pl
from jax.experimental.pallas import tpu as pltpu
from jax.sharding import Mesh
from jax.sharding import PartitionSpec as P

HEAD_DIM = 80


masked_score = -1e30


def layer_norm(values, gain, shift):
    centre = values - jnp.mean(values, axis=-1, keepdims=True)
    spread = jnp.mean(centre * centre, axis=-1, keepdims=True)
    return centre * lax.rsqrt(spread + 1e-05) * gain + shift


SEATS = 4
SLOT = 256
EXTRA = 16
MEGA = 1 << 20
LOG2E = 1.4426950408889634
CORES = ((0, 1), (1, 0))


def dot(left, right, dims):
    return lax.dot_general(
        left, right, (((dims[0],), (dims[1],)), ((), ())), preferred_element_type=jnp.float32
    )


def seat_swap(values, bits):
    return lax.ppermute(values, "seat", [(k, k ^ bits) for k in range(SEATS)])


def core_swap(values):
    return lax.ppermute(values, "core", CORES)


def plane_swap(values, bits, planes):
    return lax.ppermute(values, "tensor", [(k, k ^ bits) for k in range(planes)])


def at_index(stack, index):
    return lax.dynamic_index_in_dim(stack, index, 0, keepdims=False)


def after(value, *others):
    return lax.optimization_barrier((value, others))[0]


def leave_seat(rows, seat):
    parts = rows.reshape(SEATS, -1, rows.shape[1])
    return jnp.stack(
        [at_index(parts, seat)] + [seat_swap(at_index(parts, seat ^ r), r) for r in range(1, SEATS)]
    )


def leave_plane(got, seat, plane, planes):
    turn = seat ^ plane
    return jnp.concatenate(
        [at_index(got, turn)]
        + [plane_swap(at_index(got, turn ^ k), k, planes) for k in range(1, planes)]
    )


def from_plane(rows, seat, plane, planes):
    parts = rows.reshape(planes, -1, rows.shape[1])
    got = jnp.stack([parts[0]] + [plane_swap(parts[k], k, planes) for k in range(1, planes)])
    turn = seat ^ plane
    back = jnp.stack(
        [at_index(got, turn)] + [seat_swap(at_index(got, turn ^ r), r) for r in range(1, SEATS)]
    )
    return jnp.concatenate([at_index(back, s ^ seat) for s in range(SEATS)])


def gather_near(own):
    return own, seat_swap(own, 1), seat_swap(own, 2)


def gather_far(own, across, along):
    half = own.shape[0] // 2
    far_a, far_b = seat_swap(across[:half], 2), seat_swap(along[half:], 1)
    return jnp.concatenate([own, across, along, far_a, far_b])


def plane_gather(own):
    return gather_far(*gather_near(own))


def scatter_far(terms):
    rows = terms.shape[0] // SEATS
    half = rows // 2
    own, across, along, far = (terms[k * rows : (k + 1) * rows] for k in range(SEATS))
    far = far.astype(jnp.bfloat16)
    far_a, far_b = seat_swap(far[:half], 1), seat_swap(far[half:], 2)
    along = jnp.concatenate([along[:half] + far_a.astype(jnp.float32), along[half:]])
    across = jnp.concatenate([across[:half], across[half:] + far_b.astype(jnp.float32)])
    return own, across.astype(jnp.bfloat16), along.astype(jnp.bfloat16)


def scatter_near(own, across, along):
    along = seat_swap(along, 2).astype(jnp.float32)
    across = seat_swap(across, 1).astype(jnp.float32)
    return own + across + along


def smem():
    return pl.BlockSpec(memory_space=pltpu.SMEM)


def whole(array):
    return pl.BlockSpec(array.shape, lambda *_: (0,) * len(array.shape))


def pack_heads(sources, vectors, shifts, lengths, seat):
    rows = sources[0].shape[0]
    columns = len(sources) * HEAD_DIM
    query_shift, value_shift, up_shift = shifts
    hidden_of = up_shift.shape[1] // SEATS

    def kernel(seat_ref, length_ref, *refs):
        inputs, vector_ref, query_ref, value_ref, up_ref = refs[:4], *refs[4:8]
        outs, held, tile = refs[8:-2], refs[-2], refs[-1]
        tile[...] = jnp.zeros_like(tile)
        tile[:6, :rows] = vector_ref[...].astype(jnp.float32)
        lane = lax.broadcasted_iota(jnp.int32, (1, columns), 1)
        high, low = length_ref[0] // 8, length_ref[0] % 8
        tile[6:7, :] = jnp.where(lane == 0, high, jnp.where(lane == 1, low, 0)).astype(jnp.float32)
        for j in range(SEATS):
            of = slice(j * HEAD_DIM, (j + 1) * HEAD_DIM)
            for k in range(len(sources)):
                held[j, :rows, k * HEAD_DIM : (k + 1) * HEAD_DIM] = inputs[k][:, of]
            tile[8:9, :HEAD_DIM] = query_ref[:, of].astype(jnp.float32)
            tile[8:9, 2 * HEAD_DIM : 3 * HEAD_DIM] = value_ref[:, of].astype(jnp.float32)
            tile[9:10, :hidden_of] = up_ref[:, j * hidden_of : (j + 1) * hidden_of].astype(
                jnp.float32
            )
            held[j, rows:, :] = tile[...].astype(jnp.bfloat16)
        for r in range(SEATS):
            outs[r][...] = held[seat_ref[0] ^ r]

    piece = jax.ShapeDtypeStruct((rows + EXTRA, columns), jnp.bfloat16)
    arrays = [*sources, vectors, *shifts]
    return pl.pallas_call(
        kernel,
        out_shape=[piece] * SEATS,
        grid=(1,),
        in_specs=[smem(), smem()] + [whole(a) for a in arrays],
        out_specs=[whole(piece)] * SEATS,
        scratch_shapes=[
            pltpu.VMEM((SEATS, rows + EXTRA, columns), jnp.bfloat16),
            pltpu.VMEM((EXTRA, columns), jnp.float32),
        ],
        compiler_params=pltpu.CompilerParams(vmem_limit_bytes=16 * MEGA),
        name="pack_heads",
    )(seat, lengths, *arrays)


def pack_hidden(sources, seat):
    rows, size = sources[0].shape[0], sources[0].shape[1] // SEATS
    columns = len(sources) * size

    def kernel(seat_ref, *refs):
        inputs, outs, held = refs[: len(sources)], refs[len(sources) : -1], refs[-1]
        for j in range(SEATS):
            for k in range(len(sources)):
                held[j, :, k * size : (k + 1) * size] = inputs[k][:, j * size : (j + 1) * size]
        for r in range(SEATS):
            outs[r][...] = held[seat_ref[0] ^ r]

    piece = jax.ShapeDtypeStruct((rows, columns), jnp.bfloat16)
    return pl.pallas_call(
        kernel,
        out_shape=[piece] * SEATS,
        grid=(1,),
        in_specs=[smem()] + [whole(a) for a in sources],
        out_specs=[whole(piece)] * SEATS,
        scratch_shapes=[pltpu.VMEM((SEATS, rows, columns), jnp.bfloat16)],
        compiler_params=pltpu.CompilerParams(vmem_limit_bytes=16 * MEGA),
        name="pack_hidden",
    )(seat, *sources)


def assemble_weights(plan, gathered, seat, planes, extra):
    groups, _, tall, columns = gathered.shape
    rows = tall - extra

    def kernel(seat_ref, in_ref, *outs):
        del seat_ref
        for c in range(2):
            of = slice(c * rows, (c + 1) * rows)
            for z in range(planes):
                for k, (lane, size, stride) in enumerate(plan):
                    at = z * stride
                    outs[k][of, at : at + size] = in_ref[
                        c * planes + z, 0, :rows, lane : lane + size
                    ]
                    if size < stride:
                        outs[k][of, at + size : at + stride] = jnp.zeros(
                            (rows, stride - size), jnp.bfloat16
                        )
        if extra:
            outs[-1][0] = in_ref[:, 0, rows:, :]

    shapes = [
        jax.ShapeDtypeStruct((SEATS * 2 * rows, planes * stride), jnp.bfloat16)
        for _, _, stride in plan
    ]
    blocks = [pl.BlockSpec((2 * rows, planes * stride), lambda s, seat: (s, 0)) for _, _, stride in plan]
    if extra:
        shapes += [jax.ShapeDtypeStruct((SEATS, groups, extra, columns), jnp.bfloat16)]
        blocks += [pl.BlockSpec((1, groups, extra, columns), lambda s, seat: (s, 0, 0, 0))]
    return pl.pallas_call(
        kernel,
        out_shape=shapes,
        grid_spec=pltpu.PrefetchScalarGridSpec(
            num_scalar_prefetch=1,
            grid=(SEATS,),
            in_specs=[
                pl.BlockSpec((groups, 1, tall, columns), lambda s, seat: (0, s ^ seat[0], 0, 0))
            ],
            out_specs=blocks,
        ),
        compiler_params=pltpu.CompilerParams(vmem_limit_bytes=24 * MEGA),
        name="assemble_weights",
    )(seat, gathered)


def pack_grads(plan, columns, sources, core, planes, vectors=None, shifts=None):
    rows = sources[0].shape[0] // (2 * SEATS)
    extra = 0 if vectors is None else EXTRA
    tall = rows + extra

    def kernel(core_ref, *refs):
        inputs = refs[: len(sources)]
        for out, c in ((refs[-2], core_ref[0]), (refs[-1], 1 - core_ref[0])):
            start = pl.multiple_of(c * rows, 16)
            for z in range(planes):
                for k, stride, lane, size in plan:
                    out[z, 0, :rows, lane : lane + size] = inputs[k][
                        pl.ds(start, rows), z * stride : z * stride + size
                    ]
                if extra:
                    vec_ref, shift_ref = refs[len(sources) : len(sources) + 2]
                    out[z, 0, rows:, :] = (vec_ref[0, c] + shift_ref[z]).astype(jnp.bfloat16)

    chunk = jax.ShapeDtypeStruct((planes, SEATS, tall, columns), jnp.bfloat16)
    block = pl.BlockSpec((planes, 1, tall, columns), lambda s: (0, s, 0, 0))
    in_specs = [pl.BlockSpec((2 * rows, a.shape[1]), lambda s: (s, 0)) for a in sources]
    more = []
    if extra:
        more = [vectors, shifts]
        in_specs += [
            pl.BlockSpec((1, 2, EXTRA, columns), lambda s: (s, 0, 0, 0)),
            pl.BlockSpec((planes, EXTRA, columns), lambda s: (0, 0, 0)),
        ]
    return pl.pallas_call(
        kernel,
        out_shape=[chunk, chunk],
        grid=(SEATS,),
        in_specs=[smem()] + in_specs,
        out_specs=[block, block],
        compiler_params=pltpu.CompilerParams(vmem_limit_bytes=32 * MEGA),
        name="pack_grads",
    )(core, *sources, *more)


def finish_grads(plan, pieces, seat, extra):
    tall, columns = pieces[0].shape
    rows = tall - extra

    def kernel(seat_ref, *refs):
        outs, held = refs[SEATS:-1], refs[-1]
        for r in range(SEATS):
            held[seat_ref[0] ^ r] = refs[r][...]
        for j in range(SEATS):
            for k, (lane, size) in enumerate(plan):
                outs[k][:, j * size : (j + 1) * size] = held[j, :rows, lane : lane + size].astype(
                    jnp.float32
                )
            if extra:
                outs[-1][j] = held[j, rows:, :].astype(jnp.float32)

    shapes = [jax.ShapeDtypeStruct((rows, SEATS * size), jnp.float32) for _, size in plan]
    if extra:
        shapes += [jax.ShapeDtypeStruct((SEATS, extra, columns), jnp.float32)]
    return pl.pallas_call(
        kernel,
        out_shape=shapes,
        grid=(1,),
        in_specs=[smem()] + [whole(p) for p in pieces],
        out_specs=[whole(s) for s in shapes],
        scratch_shapes=[pltpu.VMEM((SEATS, tall, columns), jnp.bfloat16)],
        compiler_params=pltpu.CompilerParams(vmem_limit_bytes=24 * MEGA),
        name="finish_grads",
    )(seat, *pieces)


def key_shift(facts_ref, shape, planes, quarter):
    length, seat, plane = facts_ref[0], facts_ref[1], facts_ref[2]
    row = lax.broadcasted_iota(jnp.int32, shape, 0)
    sub = quarter // SEATS
    block, part, place = row // quarter, (row // sub) % planes, row % sub
    position = (plane ^ part) * quarter + (seat ^ block) * sub + place
    return jnp.where(position < length, 0.0, masked_score).astype(jnp.float32)


def attend(facts, qkv, planes, quarter):
    seq = qkv.shape[1]
    scale = HEAD_DIM ** (-0.5) * LOG2E

    def kernel(facts_ref, qkv_ref, out_ref, log_ref, shift_ref):

        @pl.when(pl.program_id(0) == 0)
        def _():
            shift_ref[...] = key_shift(facts_ref, shift_ref.shape, planes, quarter)

        keys = jnp.transpose(qkv_ref[HEAD_DIM : 2 * HEAD_DIM, :])
        values = qkv_ref[2 * HEAD_DIM : 3 * HEAD_DIM, :]
        for r in range(SEATS):
            at = slice(r * quarter, (r + 1) * quarter)
            scores = dot(keys, qkv_ref[:HEAD_DIM, at], (1, 0)) * scale + shift_ref[...]
            top = jnp.max(scores, axis=0, keepdims=True)
            expo = jnp.exp2(scores - top)
            total = jnp.sum(expo, axis=0, keepdims=True)
            context = dot(values, expo.astype(jnp.bfloat16), (1, 0)) / total
            out_ref[:, at] = context.astype(jnp.bfloat16)
            log_ref[0, :, at] = top + jnp.log2(total)

    return pl.pallas_call(
        kernel,
        out_shape=[jax.ShapeDtypeStruct((planes * HEAD_DIM, seq), jnp.bfloat16)]
        + [jax.ShapeDtypeStruct((planes, 1, seq), jnp.float32)],
        grid=(planes,),
        in_specs=[smem(), pl.BlockSpec((SLOT, seq), lambda h: (h, 0))],
        out_specs=[pl.BlockSpec((HEAD_DIM, seq), lambda h: (h, 0))]
        + [pl.BlockSpec((1, 1, seq), lambda h: (h, 0, 0))],
        scratch_shapes=[pltpu.VMEM((seq, quarter), jnp.float32)],
        compiler_params=pltpu.CompilerParams(vmem_limit_bytes=40 * MEGA),
        name="attend",
    )(facts, qkv)


def attend_grad(facts, qkv, context_grad, logs, planes, quarter):
    seq = qkv.shape[1]
    scale = HEAD_DIM ** (-0.5)

    def kernel(facts_ref, qkv_ref, grad_ref, log_ref, out_ref, shift_ref, key_acc, value_acc):
        @pl.when(pl.program_id(0) == 0)
        def _():
            shift_ref[...] = key_shift(facts_ref, shift_ref.shape, planes, quarter)

        keys = jnp.transpose(qkv_ref[HEAD_DIM : 2 * HEAD_DIM, :])
        values = jnp.transpose(qkv_ref[2 * HEAD_DIM : 3 * HEAD_DIM, :])
        for r in range(SEATS):
            at = slice(r * quarter, (r + 1) * quarter)
            queries, grad = qkv_ref[:HEAD_DIM, at], grad_ref[:, at]
            scores = dot(keys, queries, (1, 0)) * (scale * LOG2E) + shift_ref[...]
            probs = jnp.exp2(scores - log_ref[0, :, at])
            prob_grad = dot(values, grad, (1, 0))
            mean = jnp.sum(probs * prob_grad, axis=0, keepdims=True)
            score_grad = (probs * (prob_grad - mean)).astype(jnp.bfloat16)
            query_grad = dot(qkv_ref[HEAD_DIM : 2 * HEAD_DIM, :], score_grad, (1, 0))
            out_ref[:HEAD_DIM, at] = (query_grad * scale).astype(jnp.bfloat16)
            key_part = dot(queries, score_grad, (1, 1))
            value_part = dot(grad, probs.astype(jnp.bfloat16), (1, 1))
            if r == 0:
                key_acc[...] = key_part
                value_acc[...] = value_part
            else:
                key_acc[...] += key_part
                value_acc[...] += value_part
        out_ref[HEAD_DIM : 2 * HEAD_DIM, :] = (key_acc[...] * scale).astype(jnp.bfloat16)
        out_ref[2 * HEAD_DIM : 3 * HEAD_DIM, :] = value_acc[...].astype(jnp.bfloat16)
        out_ref[3 * HEAD_DIM :, :] = jnp.zeros((SLOT - 3 * HEAD_DIM, seq), jnp.bfloat16)

    return pl.pallas_call(
        kernel,
        out_shape=jax.ShapeDtypeStruct((planes * SLOT, seq), jnp.bfloat16),
        grid=(planes,),
        in_specs=[
            smem(),
            pl.BlockSpec((SLOT, seq), lambda h: (h, 0)),
            pl.BlockSpec((HEAD_DIM, seq), lambda h: (h, 0)),
            pl.BlockSpec((1, 1, seq), lambda h: (h, 0, 0)),
        ],
        out_specs=pl.BlockSpec((SLOT, seq), lambda h: (h, 0)),
        scratch_shapes=[
            pltpu.VMEM((seq, quarter), jnp.float32),
            pltpu.VMEM((HEAD_DIM, seq), jnp.float32),
            pltpu.VMEM((HEAD_DIM, seq), jnp.float32),
        ],
        compiler_params=pltpu.CompilerParams(vmem_limit_bytes=48 * MEGA),
        name="attend_grad",
    )(facts, qkv, context_grad, logs)


def norm_back(values, gain, grad):
    mean = jnp.mean(values, axis=-1, keepdims=True)
    centre = values - mean
    root = lax.rsqrt(jnp.mean(centre * centre, axis=-1, keepdims=True) + 1e-05)
    unit = centre * root
    scaled = grad * gain
    part = root * (
        scaled
        - jnp.mean(scaled, axis=-1, keepdims=True)
        - unit * jnp.mean(scaled * unit, axis=-1, keepdims=True)
    )
    return part, jnp.sum(grad * unit, axis=0), jnp.sum(grad, axis=0)


def over_cores(kept, given):
    return (kept.astype(jnp.float32) + core_swap(given).astype(jnp.float32)).astype(jnp.bfloat16)


def seat_home(owned, seat):
    return [at_index(owned, seat)] + [
        seat_swap(at_index(owned, seat ^ r), r) for r in range(1, SEATS)
    ]


def masked_scores(query_part, key_rows, valid, scale):
    scores = (
        jnp.einsum("qhe,khe->hqk", query_part, key_rows, preferred_element_type=jnp.float32) * scale
    )
    return jnp.where(valid[None, None, :], scores, masked_score)


def attend_clip(query_rows, key_rows, value_rows, valid, blocks):
    seq, heads = (query_rows.shape[0], query_rows.shape[1])
    scale = HEAD_DIM ** (-0.5)
    query_blocks = query_rows.reshape(blocks, seq // blocks, heads, HEAD_DIM)

    def one_block(query_part):
        scores = masked_scores(query_part, key_rows, valid, scale)
        top = jnp.max(scores, axis=-1, keepdims=True)
        expo = jnp.exp(scores - top)
        total = jnp.sum(expo, axis=-1, keepdims=True)
        probs = (expo / total).astype(jnp.bfloat16)
        context = jnp.einsum(
            "hqk,khe->qhe", probs, value_rows, preferred_element_type=jnp.float32
        ).astype(jnp.bfloat16)
        return (context, (top + jnp.log(total))[..., 0])

    context, log_total = lax.map(one_block, query_blocks)
    return (context.reshape(seq, heads, HEAD_DIM), log_total)


def attend_back(query_rows, key_rows, value_rows, context_grad, log_total, valid, blocks):
    seq, heads = (query_rows.shape[0], query_rows.shape[1])
    scale = HEAD_DIM ** (-0.5)
    query_blocks = query_rows.reshape(blocks, seq // blocks, heads, HEAD_DIM)
    grad_blocks = context_grad.reshape(blocks, seq // blocks, heads, HEAD_DIM)

    def one_block(carry, inputs):
        key_acc, value_acc = carry
        query_part, grad_part, lse_part = inputs
        scores = masked_scores(query_part, key_rows, valid, scale)
        probs = jnp.exp(scores - lse_part[..., None])
        value_acc = value_acc + jnp.einsum(
            "hqk,qhe->khe",
            probs.astype(jnp.bfloat16),
            grad_part,
            preferred_element_type=jnp.float32,
        )
        prob_grad = jnp.einsum(
            "qhe,khe->hqk", grad_part, value_rows, preferred_element_type=jnp.float32
        )
        centred = prob_grad - jnp.sum(probs * prob_grad, axis=-1, keepdims=True)
        score_grad = (probs * centred).astype(jnp.bfloat16)
        query_grad = (
            jnp.einsum("hqk,khe->qhe", score_grad, key_rows, preferred_element_type=jnp.float32)
            * scale
        )
        key_acc = (
            key_acc
            + jnp.einsum("hqk,qhe->khe", score_grad, query_part, preferred_element_type=jnp.float32)
            * scale
        )
        return ((key_acc, value_acc), query_grad.astype(jnp.bfloat16))

    zeros = jnp.zeros((seq, heads, HEAD_DIM), jnp.float32)
    (key_acc, value_acc), query_grad = lax.scan(
        one_block, (zeros, zeros), (query_blocks, grad_blocks, log_total)
    )
    return (
        query_grad.reshape(seq, heads, HEAD_DIM),
        key_acc.astype(jnp.bfloat16),
        value_acc.astype(jnp.bfloat16),
    )


def forward_pass(tokens, lengths, weights):
    (
        ln1_gain,
        ln1_bias,
        query_weight,
        query_bias,
        key_weight,
        value_weight,
        value_bias,
        out_weight,
        out_bias,
        ln2_gain,
        ln2_bias,
        up_weight,
        up_bias,
        down_weight,
        down_bias,
    ) = weights
    query_full, key_full, value_full, out_full, gain_one, bias_one, out_shift = (
        lax.all_gather(query_weight, "dp", axis=0, tiled=True),
        lax.all_gather(key_weight, "dp", axis=0, tiled=True),
        lax.all_gather(value_weight, "dp", axis=0, tiled=True),
        lax.all_gather(out_weight, "dp", axis=0, tiled=True),
        lax.all_gather(ln1_gain, "dp", axis=0, tiled=True),
        lax.all_gather(ln1_bias, "dp", axis=0, tiled=True),
        lax.all_gather(out_bias, "dp", axis=0, tiled=True),
    )
    gain_one = gain_one.astype(jnp.float32)
    bias_one = bias_one.astype(jnp.float32)
    rows = tokens.astype(jnp.float32)
    normed = layer_norm(rows, gain_one, bias_one).astype(jnp.bfloat16)
    normed_all = lax.all_gather(normed, "tensor", axis=1, tiled=True)
    clips, seq = (normed_all.shape[0], normed_all.shape[1])
    heads = query_full.shape[1] // HEAD_DIM
    blocks = seq // 512
    shaped = (clips, seq, heads, HEAD_DIM)
    queries = (
        (
            jnp.einsum("csd,dh->csh", normed_all, query_full, preferred_element_type=jnp.float32)
            + query_bias.astype(jnp.float32)
        )
        .astype(jnp.bfloat16)
        .reshape(shaped)
    )
    keyed = (
        jnp.einsum("csd,dh->csh", normed_all, key_full, preferred_element_type=jnp.float32)
        .astype(jnp.bfloat16)
        .reshape(shaped)
    )
    valued = (
        (
            jnp.einsum("csd,dh->csh", normed_all, value_full, preferred_element_type=jnp.float32)
            + value_bias.astype(jnp.float32)
        )
        .astype(jnp.bfloat16)
        .reshape(shaped)
    )

    def clip_attend(item):
        valid = lax.broadcasted_iota(jnp.int32, (seq,), 0) < item[3]
        return attend_clip(item[0], item[1], item[2], valid, blocks)

    context, log_total = lax.map(clip_attend, (queries, keyed, valued, lengths))
    context = context.reshape(clips, seq, heads * HEAD_DIM)
    attn_terms = jnp.einsum("csh,dh->csd", context, out_full, preferred_element_type=jnp.float32)
    attended = lax.psum_scatter(
        attn_terms.astype(jnp.bfloat16), "tensor", scatter_dimension=1, tiled=True
    ).astype(jnp.float32)
    middle = rows + attended + out_shift.astype(jnp.float32)
    up_full, down_full, gain_two, bias_two, down_shift = (
        lax.all_gather(up_weight, "dp", axis=0, tiled=True),
        lax.all_gather(down_weight, "dp", axis=0, tiled=True),
        lax.all_gather(ln2_gain, "dp", axis=0, tiled=True),
        lax.all_gather(ln2_bias, "dp", axis=0, tiled=True),
        lax.all_gather(down_bias, "dp", axis=0, tiled=True),
    )
    gain_two = gain_two.astype(jnp.float32)
    bias_two = bias_two.astype(jnp.float32)
    normed_two = layer_norm(middle, gain_two, bias_two).astype(jnp.bfloat16)
    normed_two_all = lax.all_gather(normed_two, "tensor", axis=1, tiled=True)
    hidden_pre = jnp.einsum(
        "csd,df->csf", normed_two_all, up_full, preferred_element_type=jnp.float32
    ) + up_bias.astype(jnp.float32)
    hidden = jax.nn.gelu(hidden_pre, approximate=False).astype(jnp.bfloat16)
    mlp_terms = jnp.einsum("csf,df->csd", hidden, down_full, preferred_element_type=jnp.float32)
    mixed = lax.psum_scatter(
        mlp_terms.astype(jnp.bfloat16), "tensor", scatter_dimension=1, tiled=True
    ).astype(jnp.float32)
    output = middle + mixed + down_shift.astype(jnp.float32)
    return {
        "output": output,
        "rows": rows,
        "normed_all": normed_all,
        "queries": queries,
        "keyed": keyed,
        "valued": valued,
        "context": context,
        "log_total": log_total,
        "middle": middle,
        "normed_two_all": normed_two_all,
        "hidden_pre": hidden_pre,
        "hidden": hidden,
        "query_full": query_full,
        "key_full": key_full,
        "value_full": value_full,
        "out_full": out_full,
        "up_full": up_full,
        "down_full": down_full,
        "gain_one": gain_one,
        "bias_one": bias_one,
        "gain_two": gain_two,
        "bias_two": bias_two,
        "blocks": blocks,
    }


def local(
    tokens,
    lengths,
    cotangent,
    ln1_gain,
    ln1_bias,
    query_weight,
    query_bias,
    key_weight,
    value_weight,
    value_bias,
    out_weight,
    out_bias,
    ln2_gain,
    ln2_bias,
    up_weight,
    up_bias,
    down_weight,
    down_bias,
):
    weights = (
        ln1_gain,
        ln1_bias,
        query_weight,
        query_bias,
        key_weight,
        value_weight,
        value_bias,
        out_weight,
        out_bias,
        ln2_gain,
        ln2_bias,
        up_weight,
        up_bias,
        down_weight,
        down_bias,
    )
    saved = forward_pass(tokens, lengths, weights)
    blocks = saved["blocks"]
    grad_out = cotangent.astype(jnp.float32)
    down_shift_grad = jnp.sum(grad_out, axis=(0, 1))
    grad_out_all = lax.all_gather(cotangent, "tensor", axis=1, tiled=True)
    down_grad = jnp.einsum(
        "csd,csf->df", grad_out_all, saved["hidden"], preferred_element_type=jnp.float32
    )
    hidden_grad = jnp.einsum(
        "csd,df->csf", grad_out_all, saved["down_full"], preferred_element_type=jnp.float32
    )
    gelu_pull = jax.vjp(lambda pre: jax.nn.gelu(pre, approximate=False), saved["hidden_pre"])[1]
    pre_grad = gelu_pull(hidden_grad)[0].astype(jnp.bfloat16)
    up_shift_grad = jnp.sum(pre_grad, axis=(0, 1), dtype=jnp.float32)
    up_grad = jnp.einsum(
        "csd,csf->df", saved["normed_two_all"], pre_grad, preferred_element_type=jnp.float32
    )
    up_grad_shard, down_grad_shard = (
        lax.psum_scatter(
            up_grad.astype(jnp.bfloat16), "dp", scatter_dimension=0, tiled=True
        ).astype(jnp.float32),
        lax.psum_scatter(
            down_grad.astype(jnp.bfloat16), "dp", scatter_dimension=0, tiled=True
        ).astype(jnp.float32),
    )
    normed_two_terms = jnp.einsum(
        "csf,df->csd", pre_grad, saved["up_full"], preferred_element_type=jnp.float32
    )
    normed_two_grad = lax.psum_scatter(
        normed_two_terms.astype(jnp.bfloat16), "tensor", scatter_dimension=1, tiled=True
    ).astype(jnp.float32)
    norm_pull = jax.vjp(layer_norm, saved["middle"], saved["gain_two"], saved["bias_two"])[1]
    middle_part, gain_two_grad, bias_two_grad = norm_pull(normed_two_grad)
    middle_grad = grad_out + middle_part
    out_shift_grad = jnp.sum(middle_grad, axis=(0, 1))
    middle_all = lax.all_gather(middle_grad.astype(jnp.bfloat16), "tensor", axis=1, tiled=True)
    out_grad = jnp.einsum(
        "csd,csh->dh", middle_all, saved["context"], preferred_element_type=jnp.float32
    )
    context_grad = jnp.einsum(
        "csd,dh->csh", middle_all, saved["out_full"], preferred_element_type=jnp.float32
    ).astype(jnp.bfloat16)
    queries = saved["queries"]
    clips, seq, heads = (queries.shape[0], queries.shape[1], queries.shape[2])

    def clip_back(item):
        valid = lax.broadcasted_iota(jnp.int32, (seq,), 0) < item[5]
        return attend_back(item[0], item[1], item[2], item[3], item[4], valid, blocks)

    query_grad, key_grad, value_grad = lax.map(
        clip_back,
        (
            queries,
            saved["keyed"],
            saved["valued"],
            context_grad.reshape(clips, seq, heads, HEAD_DIM),
            saved["log_total"],
            lengths,
        ),
    )
    flat = (clips, seq, heads * HEAD_DIM)
    query_grad = query_grad.reshape(flat)
    key_grad = key_grad.reshape(flat)
    value_grad = value_grad.reshape(flat)
    normed_all = saved["normed_all"]
    query_weight_grad = jnp.einsum(
        "csd,csh->dh", normed_all, query_grad, preferred_element_type=jnp.float32
    )
    key_weight_grad = jnp.einsum(
        "csd,csh->dh", normed_all, key_grad, preferred_element_type=jnp.float32
    )
    value_weight_grad = jnp.einsum(
        "csd,csh->dh", normed_all, value_grad, preferred_element_type=jnp.float32
    )
    query_shift_grad = jnp.sum(query_grad, axis=(0, 1), dtype=jnp.float32)
    value_shift_grad = jnp.sum(value_grad, axis=(0, 1), dtype=jnp.float32)
    normed_terms = (
        jnp.einsum(
            "csh,dh->csd", query_grad, saved["query_full"], preferred_element_type=jnp.float32
        )
        + jnp.einsum("csh,dh->csd", key_grad, saved["key_full"], preferred_element_type=jnp.float32)
        + jnp.einsum(
            "csh,dh->csd", value_grad, saved["value_full"], preferred_element_type=jnp.float32
        )
    )
    normed_grad = lax.psum_scatter(
        normed_terms.astype(jnp.bfloat16), "tensor", scatter_dimension=1, tiled=True
    ).astype(jnp.float32)
    first_pull = jax.vjp(layer_norm, saved["rows"], saved["gain_one"], saved["bias_one"])[1]
    tokens_part, gain_one_grad, bias_one_grad = first_pull(normed_grad)
    tokens_grad = middle_grad + tokens_part
    summed = lax.psum(
        (
            gain_one_grad,
            bias_one_grad,
            out_shift_grad,
            gain_two_grad,
            bias_two_grad,
            down_shift_grad,
        ),
        "tensor",
    )
    owned = (
        lax.psum_scatter(
            query_weight_grad.astype(jnp.bfloat16), "dp", scatter_dimension=0, tiled=True
        ).astype(jnp.float32),
        lax.psum_scatter(
            key_weight_grad.astype(jnp.bfloat16), "dp", scatter_dimension=0, tiled=True
        ).astype(jnp.float32),
        lax.psum_scatter(
            value_weight_grad.astype(jnp.bfloat16), "dp", scatter_dimension=0, tiled=True
        ).astype(jnp.float32),
        lax.psum_scatter(
            out_grad.astype(jnp.bfloat16), "dp", scatter_dimension=0, tiled=True
        ).astype(jnp.float32),
        lax.psum_scatter(
            summed[0].astype(jnp.bfloat16), "dp", scatter_dimension=0, tiled=True
        ).astype(jnp.float32),
        lax.psum_scatter(
            summed[1].astype(jnp.bfloat16), "dp", scatter_dimension=0, tiled=True
        ).astype(jnp.float32),
        lax.psum_scatter(
            summed[2].astype(jnp.bfloat16), "dp", scatter_dimension=0, tiled=True
        ).astype(jnp.float32),
        lax.psum_scatter(
            summed[3].astype(jnp.bfloat16), "dp", scatter_dimension=0, tiled=True
        ).astype(jnp.float32),
        lax.psum_scatter(
            summed[4].astype(jnp.bfloat16), "dp", scatter_dimension=0, tiled=True
        ).astype(jnp.float32),
        lax.psum_scatter(
            summed[5].astype(jnp.bfloat16), "dp", scatter_dimension=0, tiled=True
        ).astype(jnp.float32),
    )
    shared = lax.psum((query_shift_grad, value_shift_grad, up_shift_grad), "dp")
    return (
        saved["output"].astype(jnp.bfloat16),
        tokens_grad,
        owned[4],
        owned[5],
        owned[0],
        shared[0],
        owned[1],
        owned[2],
        shared[1],
        owned[3],
        owned[6],
        owned[7],
        owned[8],
        up_grad_shard,
        shared[2],
        down_grad_shard,
        owned[9],
    )


def plane_local(
    tokens,
    lengths,
    cotangent,
    ln1_gain,
    ln1_bias,
    query_weight,
    query_bias,
    key_weight,
    value_weight,
    value_bias,
    out_weight,
    out_bias,
    ln2_gain,
    ln2_bias,
    up_weight,
    up_bias,
    down_weight,
    down_bias,
):
    planes = lax.axis_size("tensor")
    core, seat = lax.axis_index("core"), lax.axis_index("seat")
    plane = lax.axis_index("tensor")
    seat_word, core_word = seat.reshape(1), core.reshape(1)
    quarter, width = tokens.shape[1], tokens.shape[2]
    rows_of = query_weight.shape[0]
    wide = query_weight.shape[1]
    hidden_of = up_weight.shape[1] // SEATS
    low, full = jnp.bfloat16, jnp.float32
    group = ("core", "tensor")

    vectors = jnp.concatenate([ln1_gain, ln1_bias, out_bias, ln2_gain, ln2_bias, down_bias])
    head_pieces = pack_heads(
        [query_weight, key_weight, value_weight, out_weight],
        vectors.reshape(6, rows_of),
        [query_bias[None], value_bias[None], up_bias[None]],
        lengths,
        seat_word,
    )
    tokens_got = leave_seat(tokens[0], seat)
    head_pieces = after(head_pieces, tokens_got)
    head_pieces = [head_pieces[0]] + [seat_swap(head_pieces[r], r) for r in range(1, SEATS)]
    head_pieces = jnp.stack(head_pieces)
    heads_around = lax.all_gather(head_pieces, group, axis=0)

    rows_low = leave_plane(tokens_got, seat, plane, planes)
    tokens_near = gather_near(rows_low)
    tokens_all = gather_far(*tokens_near)
    seq = tokens_all.shape[0]

    ff_pieces = pack_hidden([up_weight, down_weight], seat_word)
    ff_pieces = after(ff_pieces, head_pieces)
    ff_pieces = [ff_pieces[0]] + [seat_swap(ff_pieces[r], r) for r in range(1, SEATS)]
    ff_pieces = jnp.stack(ff_pieces)
    ff_around = lax.all_gather(ff_pieces, group, axis=0)

    cot_got = leave_seat(after(cotangent[0], tokens_near), seat)
    cot_low = leave_plane(after(cot_got, tokens_all, heads_around), seat, plane, planes)

    qkv_full, out_part, extra = assemble_weights(
        [(0, 3 * HEAD_DIM, SLOT), (3 * HEAD_DIM, HEAD_DIM, HEAD_DIM)],
        heads_around,
        seat_word,
        planes,
        EXTRA,
    )
    vectors = extra[:, ::planes, :6, :rows_of].astype(full)
    gain_one, bias_one, out_shift, gain_two, bias_two, down_shift = (
        vectors[:, :, k].reshape(width) for k in range(6)
    )
    qkv_shift = jnp.pad(
        extra[0, :planes, 8, : 3 * HEAD_DIM].astype(full), ((0, 0), (0, SLOT - 3 * HEAD_DIM))
    ).reshape(planes * SLOT, 1)
    up_shift = extra[0, :planes, 9, :hidden_of].astype(full).reshape(planes * hidden_of)
    size = lax.dynamic_index_in_dim(at_index(extra, plane), core * planes, 0, keepdims=False)
    length = (8.0 * size[6, 0].astype(full) + size[6, 1].astype(full)).astype(jnp.int32)
    facts = jnp.stack([length, seat, plane])

    rows = rows_low.astype(full)
    normed_all = layer_norm(tokens_all.astype(full), gain_one, bias_one).astype(low)
    qkv = (dot(qkv_full, normed_all, (0, 1)) + qkv_shift).astype(low)
    qkv, cot_low = lax.optimization_barrier((qkv, cot_low))
    cot_near = gather_near(cot_low)
    context, logs = attend(facts, qkv, planes, quarter)
    context, cot_near = lax.optimization_barrier((context, cot_near))
    cot_all = gather_far(*cot_near)
    attended = scatter_near(*scatter_far(dot(context, out_part, (0, 1))))
    middle = rows + attended + out_shift
    normed_two = layer_norm(middle, gain_two, bias_two).astype(low)
    normed_two_all = plane_gather(normed_two)
    up_full, down_full = assemble_weights(
        [(0, hidden_of, hidden_of), (hidden_of, hidden_of, hidden_of)],
        ff_around,
        seat_word,
        planes,
        0,
    )
    hidden_grad = dot(cot_all, down_full, (1, 0))
    hidden_pre = dot(normed_two_all, up_full, (1, 0)) + up_shift
    normal = 0.5 * (1.0 + lax.erf(hidden_pre * (0.5**0.5)))
    slope = normal + hidden_pre * (jnp.exp(-0.5 * hidden_pre * hidden_pre) * (0.5 / jnp.pi) ** 0.5)
    hidden = (hidden_pre * normal).astype(low)
    pre_grad = (hidden_grad * slope).astype(low)

    terms = dot(pre_grad, up_full, (1, 1))
    pre_grad_later = after(pre_grad, terms)
    own, across, along = scatter_far(terms)
    up_grad = dot(normed_two_all, pre_grad_later, (0, 0)).astype(low)
    up_shift_grad = jnp.sum(pre_grad_later, axis=0, dtype=full).reshape(planes, hidden_of)
    hidden_later = after(hidden, up_grad, across, along)
    down_grad = dot(cot_all, hidden_later, (0, 0)).astype(low)
    grad_out = cot_low.astype(full)

    ff_kept, ff_given = pack_grads(
        [(0, hidden_of, 0, hidden_of), (1, hidden_of, hidden_of, hidden_of)],
        2 * hidden_of,
        [up_grad, down_grad],
        core_word,
        planes,
    )
    normed_two_grad = after(scatter_near(own, across, along), ff_given)
    middle_part, gain_two_grad, bias_two_grad = norm_back(middle, gain_two, normed_two_grad)
    middle_grad = grad_out + middle_part
    middle_low = middle_grad.astype(low)
    middle_all = plane_gather(middle_low)
    ff_both = over_cores(ff_kept, ff_given)
    ff_owned = lax.psum_scatter(ff_both, "tensor", scatter_dimension=0, tiled=False)
    mixed_terms = dot(after(hidden, middle_low, ff_both), down_full, (1, 1))
    middle_all, context, mixed_terms = lax.optimization_barrier(
        (middle_all, context, mixed_terms)
    )
    mixed = scatter_far(mixed_terms)

    context_grad = dot(out_part, middle_all, (0, 1)).astype(low)
    qkv_grad = attend_grad(facts, qkv, context_grad, logs, planes, quarter)
    qkv_grad, mixed = lax.optimization_barrier((qkv_grad, mixed))
    terms = dot(qkv_grad, qkv_full, (0, 1))
    qkv_grad_later, middle_later = after((qkv_grad, middle_all), terms)
    normed_grad = scatter_near(*scatter_far(terms))
    qkv_weight_grad = dot(normed_all, qkv_grad_later, (0, 1)).astype(low)
    out_grad = dot(middle_later, context, (0, 1)).astype(low)
    qkv_shift_grad = jnp.sum(qkv_grad_later, axis=1, dtype=full).reshape(planes, SLOT)
    columns = 4 * HEAD_DIM
    sums = [gain_two_grad, bias_two_grad, jnp.sum(middle_grad, axis=0), jnp.sum(grad_out, axis=0)]
    by_owner = jnp.stack(sums).reshape(len(sums), SEATS, 2, rows_of).transpose(1, 2, 0, 3)
    shifts = jnp.stack(
        [jnp.pad(qkv_shift_grad, ((0, 0), (0, columns - SLOT))), up_shift_grad], axis=1
    )
    heads_kept, heads_given = pack_grads(
        [(0, SLOT, 0, 3 * HEAD_DIM), (1, HEAD_DIM, 3 * HEAD_DIM, HEAD_DIM)],
        columns,
        [qkv_weight_grad, out_grad],
        core_word,
        planes,
        jnp.pad(by_owner, ((0, 0), (0, 0), (0, EXTRA - len(sums)), (0, columns - rows_of))),
        jnp.pad(shifts, ((0, 0), (8, EXTRA - 10), (0, 0))),
    )
    heads_both, ff_owned = lax.optimization_barrier(
        (over_cores(heads_kept, heads_given), ff_owned)
    )
    heads_owned = lax.psum_scatter(heads_both, "tensor", scatter_dimension=0, tiled=False)
    normed_grad = after(normed_grad, heads_given)
    mixed = scatter_near(*after(mixed, normed_grad))
    output = (middle + mixed + down_shift).astype(low)
    tokens_part, gain_one_grad, bias_one_grad = norm_back(rows, gain_one, normed_grad)
    tokens_grad = (middle_grad + tokens_part).astype(low)
    tokens_grad_home = from_plane(tokens_grad, seat, plane, planes)
    output_home = from_plane(output, seat, plane, planes)
    ones = jnp.concatenate([gain_one_grad, bias_one_grad])
    ones = ones + core_swap(ones)
    for bits in (1, 2):
        ones = ones + seat_swap(ones, bits)
    for bits in (1, 2):
        ones = ones + plane_swap(ones, bits, planes)
    ones = lax.dynamic_slice_in_dim(
        ones.reshape(2, width), (2 * seat + core) * rows_of, rows_of, 1
    )

    up_home, down_home = finish_grads(
        [(0, hidden_of), (hidden_of, hidden_of)], seat_home(ff_owned, seat), seat_word, 0
    )
    query_home, key_home, value_home, out_home, rest = finish_grads(
        [(k * HEAD_DIM, HEAD_DIM) for k in range(4)],
        seat_home(heads_owned, seat),
        seat_word,
        EXTRA,
    )
    sums = jnp.sum(rest[:, :4, :rows_of], axis=0)
    query_shift_home = rest[:, 8, :HEAD_DIM].reshape(wide)
    value_shift_home = rest[:, 8, 2 * HEAD_DIM : 3 * HEAD_DIM].reshape(wide)
    up_shift_home = rest[:, 9, :hidden_of].reshape(SEATS * hidden_of)

    return (
        output_home[None],
        tokens_grad_home[None].astype(full),
        ones[0],
        ones[1],
        query_home,
        query_shift_home,
        key_home,
        value_home,
        value_shift_home,
        out_home,
        sums[2],
        sums[0],
        sums[1],
        up_home,
        up_shift_home,
        down_home,
        sums[3],
    )


def specs(rows, columns):
    both = (P(rows, columns, None), P(rows), P(rows, columns), P(columns))
    cube, first, matrix, second = both
    ins = (cube, first, cube, first, first, matrix, second, matrix, matrix, second, matrix)
    ins += (first, first, first, matrix, second, matrix, first)
    outs = (cube, cube, first, first, matrix, second, matrix, matrix, second, matrix)
    outs += (first, first, first, matrix, second, matrix, first)
    return ins, outs


def solution(mesh):
    step, rows = local, "dp"
    if mesh.shape["dp"] == 2 * SEATS and mesh.shape["tensor"] == SEATS:
        devices = mesh.devices.reshape(SEATS, 2, SEATS)
        step, rows, mesh = plane_local, ("seat", "core"), Mesh(devices, ("seat", "core", "tensor"))
    ins, outs = specs(rows, "tensor")
    return jax.shard_map(step, mesh=mesh, in_specs=ins, out_specs=outs, check_vma=False)
```

```python
import jax
import jax.numpy as jnp
from jax import lax
from jax.experimental import pallas as pl
from jax.experimental.pallas import tpu as pltpu
from jax.sharding import Mesh
from jax.sharding import PartitionSpec as P

HEAD_DIM = 80


masked_score = -1e30


def layer_norm(values, gain, shift):
    centre = values - jnp.mean(values, axis=-1, keepdims=True)
    spread = jnp.mean(centre * centre, axis=-1, keepdims=True)
    return centre * lax.rsqrt(spread + 1e-05) * gain + shift


SEATS = 4
SLOT = 256
EXTRA = 16
FOLD = 2
MEGA = 1 << 20
LOG2E = 1.4426950408889634
CORES = ((0, 1), (1, 0))


def dot(left, right, dims):
    return lax.dot_general(
        left, right, (((dims[0],), (dims[1],)), ((), ())), preferred_element_type=jnp.float32
    )


def seat_swap(values, bits):
    return lax.ppermute(values, "seat", [(k, k ^ bits) for k in range(SEATS)])


def core_swap(values):
    return lax.ppermute(values, "core", CORES)


def plane_swap(values, bits, planes):
    return lax.ppermute(values, "tensor", [(k, k ^ bits) for k in range(planes)])


def at_index(stack, index):
    return lax.dynamic_index_in_dim(stack, index, 0, keepdims=False)


def after(value, *others):
    return lax.optimization_barrier((value, others))[0]


def leave_seat(parts, seat):
    return jnp.stack(
        [at_index(parts, seat)] + [seat_swap(at_index(parts, seat ^ r), r) for r in range(1, SEATS)]
    )


def leave_plane(got, seat, plane, planes):
    turn = seat ^ plane
    return jnp.stack(
        [at_index(got, turn)]
        + [plane_swap(at_index(got, turn ^ k), k, planes) for k in range(1, planes)]
    )


def enter_plane(parts, planes):
    return jnp.stack([parts[0]] + [plane_swap(parts[k], k, planes) for k in range(1, planes)])


def enter_seat(got, seat, plane):
    turn = seat ^ plane
    back = jnp.stack(
        [at_index(got, turn)] + [seat_swap(at_index(got, turn ^ r), r) for r in range(1, SEATS)]
    )
    return jnp.stack([at_index(back, s ^ seat) for s in range(SEATS)])


def gather_near(own):
    return own, seat_swap(own, 1), seat_swap(own, 2)


def gather_far(own, across, along):
    half = own.shape[0] // 2
    return own, across, along, seat_swap(across[:half], 2), seat_swap(along[half:], 1)


def scatter_far(terms):
    rows = terms.shape[0] // SEATS
    half = rows // 2
    own, across, along, far = (terms[k * rows : (k + 1) * rows] for k in range(SEATS))
    far = far.astype(jnp.bfloat16)
    far_a, far_b = seat_swap(far[:half], 1), seat_swap(far[half:], 2)
    along = jnp.concatenate([along[:half] + far_a.astype(jnp.float32), along[half:]])
    across = jnp.concatenate([across[:half], across[half:] + far_b.astype(jnp.float32)])
    return own, across.astype(jnp.bfloat16), along.astype(jnp.bfloat16)


def scatter_near(own, across, along):
    along = seat_swap(along, 2).astype(jnp.float32)
    across = seat_swap(across, 1).astype(jnp.float32)
    return own + across + along


def smem():
    return pl.BlockSpec(memory_space=pltpu.SMEM)


def whole(array):
    return pl.BlockSpec(array.shape, lambda *_: (0,) * len(array.shape))


def pack_heads(sources, vectors, shifts, lengths, seat):
    rows = sources[0].shape[0]
    columns = len(sources) * HEAD_DIM
    short, few = rows // FOLD, EXTRA // FOLD
    query_shift, value_shift, up_shift = shifts
    hidden_of = up_shift.shape[1] // SEATS

    def kernel(seat_ref, length_ref, *refs):
        inputs, vector_ref, query_ref, value_ref, up_ref = refs[:4], *refs[4:8]
        outs, held, tile = refs[8:-2], refs[-2], refs[-1]
        tile[...] = jnp.zeros_like(tile)
        tile[:6, :rows] = vector_ref[...].astype(jnp.float32)
        lane = lax.broadcasted_iota(jnp.int32, (1, columns), 1)
        high, low = length_ref[0] // 8, length_ref[0] % 8
        tile[6:7, :] = jnp.where(lane == 0, high, jnp.where(lane == 1, low, 0)).astype(jnp.float32)
        for j in range(SEATS):
            of = slice(j * HEAD_DIM, (j + 1) * HEAD_DIM)
            for k in range(len(sources)):
                for f in range(FOLD):
                    at = f * columns + k * HEAD_DIM
                    held[j, :short, at : at + HEAD_DIM] = inputs[k][
                        f * short : (f + 1) * short, of
                    ]
            tile[8:9, :HEAD_DIM] = query_ref[:, of].astype(jnp.float32)
            tile[8:9, 2 * HEAD_DIM : 3 * HEAD_DIM] = value_ref[:, of].astype(jnp.float32)
            tile[9:10, :hidden_of] = up_ref[:, j * hidden_of : (j + 1) * hidden_of].astype(
                jnp.float32
            )
            for f in range(FOLD):
                held[j, short:, f * columns : (f + 1) * columns] = tile[
                    f * few : (f + 1) * few, :
                ].astype(jnp.bfloat16)
        for r in range(SEATS):
            outs[r][...] = held[seat_ref[0] ^ r]

    piece = jax.ShapeDtypeStruct((short + few, FOLD * columns), jnp.bfloat16)
    arrays = [*sources, vectors, *shifts]
    return pl.pallas_call(
        kernel,
        out_shape=[piece] * SEATS,
        grid=(1,),
        in_specs=[smem(), smem()] + [whole(a) for a in arrays],
        out_specs=[whole(piece)] * SEATS,
        scratch_shapes=[
            pltpu.VMEM((SEATS, short + few, FOLD * columns), jnp.bfloat16),
            pltpu.VMEM((EXTRA, columns), jnp.float32),
        ],
        compiler_params=pltpu.CompilerParams(vmem_limit_bytes=4 * MEGA),
        name="pack_heads",
    )(seat, lengths, *arrays)


def pack_hidden(sources, seat):
    rows, size = sources[0].shape[0], sources[0].shape[1] // SEATS
    columns = len(sources) * size

    def kernel(seat_ref, *refs):
        inputs, outs, held = refs[: len(sources)], refs[len(sources) : -1], refs[-1]
        for j in range(SEATS):
            for k in range(len(sources)):
                held[j, :, k * size : (k + 1) * size] = inputs[k][:, j * size : (j + 1) * size]
        for r in range(SEATS):
            outs[r][...] = held[seat_ref[0] ^ r]

    piece = jax.ShapeDtypeStruct((rows, columns), jnp.bfloat16)
    return pl.pallas_call(
        kernel,
        out_shape=[piece] * SEATS,
        grid=(1,),
        in_specs=[smem()] + [whole(a) for a in sources],
        out_specs=[whole(piece)] * SEATS,
        scratch_shapes=[pltpu.VMEM((SEATS, rows, columns), jnp.bfloat16)],
        compiler_params=pltpu.CompilerParams(vmem_limit_bytes=6 * MEGA),
        name="pack_hidden",
    )(seat, *sources)


def assemble_weights(plan, gathered, seat, planes, extra, fold):
    groups, _, tall, columns = gathered.shape
    columns, few = columns // fold, extra // fold
    short = tall - few
    rows = short * fold

    def kernel(seat_ref, in_ref, *outs):
        del seat_ref
        for c in range(2):
            of = slice(c * rows, (c + 1) * rows)
            for z in range(planes):
                for k, (lane, size, stride) in enumerate(plan):
                    at = z * stride
                    for f in range(fold):
                        start = f * columns + lane
                        outs[k][c * rows + f * short : c * rows + (f + 1) * short, at : at + size] = (
                            in_ref[c * planes + z, 0, :short, start : start + size]
                        )
                    if size < stride:
                        outs[k][of, at + size : at + stride] = jnp.zeros(
                            (rows, stride - size), jnp.bfloat16
                        )
        if extra:
            for f in range(fold):
                outs[-1][0, :, f * few : (f + 1) * few, :] = in_ref[
                    :, 0, short:, f * columns : (f + 1) * columns
                ].astype(jnp.float32)

    shapes = [
        jax.ShapeDtypeStruct((SEATS * 2 * rows, planes * stride), jnp.bfloat16)
        for _, _, stride in plan
    ]
    blocks = [pl.BlockSpec((2 * rows, planes * stride), lambda s, seat: (s, 0)) for _, _, stride in plan]
    if extra:
        shapes += [jax.ShapeDtypeStruct((SEATS, groups, extra, columns), jnp.float32)]
        blocks += [pl.BlockSpec((1, groups, extra, columns), lambda s, seat: (s, 0, 0, 0))]
    return pl.pallas_call(
        kernel,
        out_shape=shapes,
        grid_spec=pltpu.PrefetchScalarGridSpec(
            num_scalar_prefetch=1,
            grid=(SEATS,),
            in_specs=[
                pl.BlockSpec((groups, 1, tall, fold * columns), lambda s, seat: (0, s ^ seat[0], 0, 0))
            ],
            out_specs=blocks,
        ),
        compiler_params=pltpu.CompilerParams(vmem_limit_bytes=12 * MEGA),
        name="assemble_weights",
    )(seat, gathered)


def pack_grads(plan, columns, sources, core, planes, fold=1, vectors=None, shifts=None):
    rows = sources[0].shape[0] // (2 * SEATS)
    extra = 0 if vectors is None else EXTRA
    short, few = rows // fold, extra // fold
    tall = short + few

    def kernel(core_ref, *refs):
        inputs = refs[: len(sources)]
        for out, c in ((refs[-2], core_ref[0]), (refs[-1], 1 - core_ref[0])):
            for z in range(planes):
                for f in range(fold):
                    start = pl.multiple_of(c * rows + f * short, 16)
                    for k, stride, lane, size in plan:
                        at = f * columns + lane
                        out[z, 0, :short, at : at + size] = inputs[k][
                            pl.ds(start, short), z * stride : z * stride + size
                        ]
                    if extra:
                        vec_ref, shift_ref = refs[len(sources) : len(sources) + 2]
                        of = slice(f * few, (f + 1) * few)
                        out[z, 0, short:, f * columns : (f + 1) * columns] = (
                            vec_ref[0, c, of, :] + shift_ref[z, of, :]
                        ).astype(jnp.bfloat16)

    chunk = jax.ShapeDtypeStruct((planes, SEATS, tall, fold * columns), jnp.bfloat16)
    block = pl.BlockSpec((planes, 1, tall, fold * columns), lambda s: (0, s, 0, 0))
    in_specs = [pl.BlockSpec((2 * rows, a.shape[1]), lambda s: (s, 0)) for a in sources]
    more = []
    if extra:
        more = [vectors, shifts]
        in_specs += [
            pl.BlockSpec((1, 2, EXTRA, columns), lambda s: (s, 0, 0, 0)),
            pl.BlockSpec((planes, EXTRA, columns), lambda s: (0, 0, 0)),
        ]
    return pl.pallas_call(
        kernel,
        out_shape=[chunk, chunk],
        grid=(SEATS,),
        in_specs=[smem()] + in_specs,
        out_specs=[block, block],
        compiler_params=pltpu.CompilerParams(vmem_limit_bytes=12 * MEGA),
        name="pack_grads",
    )(core, *sources, *more)


def finish_grads(plan, pieces, seat, extra, fold):
    tall, columns = pieces[0].shape
    columns, few = columns // fold, extra // fold
    short = tall - few
    rows = short * fold

    def kernel(seat_ref, *refs):
        outs, held = refs[SEATS:-1], refs[-1]
        for r in range(SEATS):
            held[seat_ref[0] ^ r] = refs[r][...]
        for j in range(SEATS):
            for k, (lane, size) in enumerate(plan):
                for f in range(fold):
                    at = f * columns + lane
                    outs[k][f * short : (f + 1) * short, j * size : (j + 1) * size] = held[
                        j, :short, at : at + size
                    ].astype(jnp.float32)
            for f in range(fold if extra else 0):
                outs[-1][j, f * few : (f + 1) * few, :] = held[
                    j, short:, f * columns : (f + 1) * columns
                ].astype(jnp.float32)

    shapes = [jax.ShapeDtypeStruct((rows, SEATS * size), jnp.float32) for _, size in plan]
    if extra:
        shapes += [jax.ShapeDtypeStruct((SEATS, extra, columns), jnp.float32)]
    return pl.pallas_call(
        kernel,
        out_shape=shapes,
        grid=(1,),
        in_specs=[smem()] + [whole(p) for p in pieces],
        out_specs=[whole(s) for s in shapes],
        scratch_shapes=[pltpu.VMEM((SEATS, tall, fold * columns), jnp.bfloat16)],
        compiler_params=pltpu.CompilerParams(vmem_limit_bytes=8 * MEGA),
        name="finish_grads",
    )(seat, *pieces)


def key_shift(facts_ref, shape, planes, quarter):
    length, seat, plane = facts_ref[0], facts_ref[1], facts_ref[2]
    row = lax.broadcasted_iota(jnp.int32, shape, 0)
    sub = quarter // SEATS
    block, part, place = row // quarter, (row // sub) % planes, row % sub
    position = (plane ^ part) * quarter + (seat ^ block) * sub + place
    return jnp.where(position < length, 0.0, masked_score).astype(jnp.float32)


def attend(facts, qkv, planes, quarter):
    seq = qkv.shape[1]
    scale = HEAD_DIM ** (-0.5) * LOG2E

    def kernel(facts_ref, qkv_ref, out_ref, log_ref, shift_ref):

        @pl.when(pl.program_id(0) == 0)
        def _():
            shift_ref[...] = key_shift(facts_ref, shift_ref.shape, planes, quarter)

        keys = jnp.transpose(qkv_ref[HEAD_DIM : 2 * HEAD_DIM, :])
        values = qkv_ref[2 * HEAD_DIM : 3 * HEAD_DIM, :]
        for r in range(SEATS):
            at = slice(r * quarter, (r + 1) * quarter)
            scores = dot(keys, qkv_ref[:HEAD_DIM, at], (1, 0)) * scale + shift_ref[...]
            top = jnp.max(scores, axis=0, keepdims=True)
            expo = jnp.exp2(scores - top)
            total = jnp.sum(expo, axis=0, keepdims=True)
            context = dot(values, expo.astype(jnp.bfloat16), (1, 0)) / total
            out_ref[:, at] = context.astype(jnp.bfloat16)
            log_ref[0, :, at] = top + jnp.log2(total)

    return pl.pallas_call(
        kernel,
        out_shape=[jax.ShapeDtypeStruct((planes * HEAD_DIM, seq), jnp.bfloat16)]
        + [jax.ShapeDtypeStruct((planes, 1, seq), jnp.float32)],
        grid=(planes,),
        in_specs=[smem(), pl.BlockSpec((SLOT, seq), lambda h: (h, 0))],
        out_specs=[pl.BlockSpec((HEAD_DIM, seq), lambda h: (h, 0))]
        + [pl.BlockSpec((1, 1, seq), lambda h: (h, 0, 0))],
        scratch_shapes=[pltpu.VMEM((seq, quarter), jnp.float32)],
        compiler_params=pltpu.CompilerParams(vmem_limit_bytes=24 * MEGA),
        name="attend",
    )(facts, qkv)


def attend_grad(facts, qkv, context_grad, logs, planes, quarter, first, heads, begun=None):
    seq = qkv.shape[1]
    scale = HEAD_DIM ** (-0.5)

    def kernel(facts_ref, qkv_ref, grad_ref, log_ref, *refs):
        out_ref, shift_ref, key_acc, value_acc = refs[-4:]

        @pl.when(pl.program_id(0) == 0)
        def _():
            shift_ref[...] = key_shift(facts_ref, shift_ref.shape, planes, quarter)

        keys = jnp.transpose(qkv_ref[HEAD_DIM : 2 * HEAD_DIM, :])
        values = jnp.transpose(qkv_ref[2 * HEAD_DIM : 3 * HEAD_DIM, :])
        for r in range(SEATS):
            at = slice(r * quarter, (r + 1) * quarter)
            queries, grad = qkv_ref[:HEAD_DIM, at], grad_ref[:, at]
            scores = dot(keys, queries, (1, 0)) * (scale * LOG2E) + shift_ref[...]
            probs = jnp.exp2(scores - log_ref[0, :, at])
            prob_grad = dot(values, grad, (1, 0))
            mean = jnp.sum(probs * prob_grad, axis=0, keepdims=True)
            score_grad = (probs * (prob_grad - mean)).astype(jnp.bfloat16)
            query_grad = dot(qkv_ref[HEAD_DIM : 2 * HEAD_DIM, :], score_grad, (1, 0))
            out_ref[:HEAD_DIM, at] = (query_grad * scale).astype(jnp.bfloat16)
            key_part = dot(queries, score_grad, (1, 1))
            value_part = dot(grad, probs.astype(jnp.bfloat16), (1, 1))
            if r == 0:
                key_acc[...] = key_part
                value_acc[...] = value_part
            else:
                key_acc[...] += key_part
                value_acc[...] += value_part
        out_ref[HEAD_DIM : 2 * HEAD_DIM, :] = (key_acc[...] * scale).astype(jnp.bfloat16)
        out_ref[2 * HEAD_DIM : 3 * HEAD_DIM, :] = value_acc[...].astype(jnp.bfloat16)
        out_ref[3 * HEAD_DIM :, :] = jnp.zeros((SLOT - 3 * HEAD_DIM, seq), jnp.bfloat16)

    more = [] if begun is None else [begun]
    more_specs = [pl.BlockSpec(memory_space=pl.ANY) for _ in more]
    return pl.pallas_call(
        kernel,
        out_shape=jax.ShapeDtypeStruct((planes * SLOT, seq), jnp.bfloat16),
        grid=(heads,),
        in_specs=[
            smem(),
            pl.BlockSpec((SLOT, seq), lambda h: (first + h, 0)),
            pl.BlockSpec((HEAD_DIM, seq), lambda h: (first + h, 0)),
            pl.BlockSpec((1, 1, seq), lambda h: (first + h, 0, 0)),
            *more_specs,
        ],
        out_specs=pl.BlockSpec((SLOT, seq), lambda h: (first + h, 0)),
        scratch_shapes=[
            pltpu.VMEM((seq, quarter), jnp.float32),
            pltpu.VMEM((HEAD_DIM, seq), jnp.float32),
            pltpu.VMEM((HEAD_DIM, seq), jnp.float32),
        ],
        compiler_params=pltpu.CompilerParams(vmem_limit_bytes=32 * MEGA),
        name="attend_grad",
        input_output_aliases={4: 0} if more else {},
    )(facts, qkv, context_grad, logs, *more)


def norm_back(values, gain, grad):
    mean = jnp.mean(values, axis=-1, keepdims=True)
    centre = values - mean
    root = lax.rsqrt(jnp.mean(centre * centre, axis=-1, keepdims=True) + 1e-05)
    unit = centre * root
    scaled = grad * gain
    part = root * (
        scaled
        - jnp.mean(scaled, axis=-1, keepdims=True)
        - unit * jnp.mean(scaled * unit, axis=-1, keepdims=True)
    )
    return part, jnp.sum(grad * unit, axis=0), jnp.sum(grad, axis=0)


def over_cores(kept, given):
    return (kept.astype(jnp.float32) + core_swap(given).astype(jnp.float32)).astype(jnp.bfloat16)


def seat_home(owned, seat):
    return [at_index(owned, seat)] + [
        seat_swap(at_index(owned, seat ^ r), r) for r in range(1, SEATS)
    ]


def masked_scores(query_part, key_rows, valid, scale):
    scores = (
        jnp.einsum("qhe,khe->hqk", query_part, key_rows, preferred_element_type=jnp.float32) * scale
    )
    return jnp.where(valid[None, None, :], scores, masked_score)


def attend_clip(query_rows, key_rows, value_rows, valid, blocks):
    seq, heads = (query_rows.shape[0], query_rows.shape[1])
    scale = HEAD_DIM ** (-0.5)
    query_blocks = query_rows.reshape(blocks, seq // blocks, heads, HEAD_DIM)

    def one_block(query_part):
        scores = masked_scores(query_part, key_rows, valid, scale)
        top = jnp.max(scores, axis=-1, keepdims=True)
        expo = jnp.exp(scores - top)
        total = jnp.sum(expo, axis=-1, keepdims=True)
        probs = (expo / total).astype(jnp.bfloat16)
        context = jnp.einsum(
            "hqk,khe->qhe", probs, value_rows, preferred_element_type=jnp.float32
        ).astype(jnp.bfloat16)
        return (context, (top + jnp.log(total))[..., 0])

    context, log_total = lax.map(one_block, query_blocks)
    return (context.reshape(seq, heads, HEAD_DIM), log_total)


def attend_back(query_rows, key_rows, value_rows, context_grad, log_total, valid, blocks):
    seq, heads = (query_rows.shape[0], query_rows.shape[1])
    scale = HEAD_DIM ** (-0.5)
    query_blocks = query_rows.reshape(blocks, seq // blocks, heads, HEAD_DIM)
    grad_blocks = context_grad.reshape(blocks, seq // blocks, heads, HEAD_DIM)

    def one_block(carry, inputs):
        key_acc, value_acc = carry
        query_part, grad_part, lse_part = inputs
        scores = masked_scores(query_part, key_rows, valid, scale)
        probs = jnp.exp(scores - lse_part[..., None])
        value_acc = value_acc + jnp.einsum(
            "hqk,qhe->khe",
            probs.astype(jnp.bfloat16),
            grad_part,
            preferred_element_type=jnp.float32,
        )
        prob_grad = jnp.einsum(
            "qhe,khe->hqk", grad_part, value_rows, preferred_element_type=jnp.float32
        )
        centred = prob_grad - jnp.sum(probs * prob_grad, axis=-1, keepdims=True)
        score_grad = (probs * centred).astype(jnp.bfloat16)
        query_grad = (
            jnp.einsum("hqk,khe->qhe", score_grad, key_rows, preferred_element_type=jnp.float32)
            * scale
        )
        key_acc = (
            key_acc
            + jnp.einsum("hqk,qhe->khe", score_grad, query_part, preferred_element_type=jnp.float32)
            * scale
        )
        return ((key_acc, value_acc), query_grad.astype(jnp.bfloat16))

    zeros = jnp.zeros((seq, heads, HEAD_DIM), jnp.float32)
    (key_acc, value_acc), query_grad = lax.scan(
        one_block, (zeros, zeros), (query_blocks, grad_blocks, log_total)
    )
    return (
        query_grad.reshape(seq, heads, HEAD_DIM),
        key_acc.astype(jnp.bfloat16),
        value_acc.astype(jnp.bfloat16),
    )


def forward_pass(tokens, lengths, weights):
    (
        ln1_gain,
        ln1_bias,
        query_weight,
        query_bias,
        key_weight,
        value_weight,
        value_bias,
        out_weight,
        out_bias,
        ln2_gain,
        ln2_bias,
        up_weight,
        up_bias,
        down_weight,
        down_bias,
    ) = weights
    query_full, key_full, value_full, out_full, gain_one, bias_one, out_shift = (
        lax.all_gather(query_weight, "dp", axis=0, tiled=True),
        lax.all_gather(key_weight, "dp", axis=0, tiled=True),
        lax.all_gather(value_weight, "dp", axis=0, tiled=True),
        lax.all_gather(out_weight, "dp", axis=0, tiled=True),
        lax.all_gather(ln1_gain, "dp", axis=0, tiled=True),
        lax.all_gather(ln1_bias, "dp", axis=0, tiled=True),
        lax.all_gather(out_bias, "dp", axis=0, tiled=True),
    )
    gain_one = gain_one.astype(jnp.float32)
    bias_one = bias_one.astype(jnp.float32)
    rows = tokens.astype(jnp.float32)
    normed = layer_norm(rows, gain_one, bias_one).astype(jnp.bfloat16)
    normed_all = lax.all_gather(normed, "tensor", axis=1, tiled=True)
    clips, seq = (normed_all.shape[0], normed_all.shape[1])
    heads = query_full.shape[1] // HEAD_DIM
    blocks = seq // 512
    shaped = (clips, seq, heads, HEAD_DIM)
    queries = (
        (
            jnp.einsum("csd,dh->csh", normed_all, query_full, preferred_element_type=jnp.float32)
            + query_bias.astype(jnp.float32)
        )
        .astype(jnp.bfloat16)
        .reshape(shaped)
    )
    keyed = (
        jnp.einsum("csd,dh->csh", normed_all, key_full, preferred_element_type=jnp.float32)
        .astype(jnp.bfloat16)
        .reshape(shaped)
    )
    valued = (
        (
            jnp.einsum("csd,dh->csh", normed_all, value_full, preferred_element_type=jnp.float32)
            + value_bias.astype(jnp.float32)
        )
        .astype(jnp.bfloat16)
        .reshape(shaped)
    )

    def clip_attend(item):
        valid = lax.broadcasted_iota(jnp.int32, (seq,), 0) < item[3]
        return attend_clip(item[0], item[1], item[2], valid, blocks)

    context, log_total = lax.map(clip_attend, (queries, keyed, valued, lengths))
    context = context.reshape(clips, seq, heads * HEAD_DIM)
    attn_terms = jnp.einsum("csh,dh->csd", context, out_full, preferred_element_type=jnp.float32)
    attended = lax.psum_scatter(
        attn_terms.astype(jnp.bfloat16), "tensor", scatter_dimension=1, tiled=True
    ).astype(jnp.float32)
    middle = rows + attended + out_shift.astype(jnp.float32)
    up_full, down_full, gain_two, bias_two, down_shift = (
        lax.all_gather(up_weight, "dp", axis=0, tiled=True),
        lax.all_gather(down_weight, "dp", axis=0, tiled=True),
        lax.all_gather(ln2_gain, "dp", axis=0, tiled=True),
        lax.all_gather(ln2_bias, "dp", axis=0, tiled=True),
        lax.all_gather(down_bias, "dp", axis=0, tiled=True),
    )
    gain_two = gain_two.astype(jnp.float32)
    bias_two = bias_two.astype(jnp.float32)
    normed_two = layer_norm(middle, gain_two, bias_two).astype(jnp.bfloat16)
    normed_two_all = lax.all_gather(normed_two, "tensor", axis=1, tiled=True)
    hidden_pre = jnp.einsum(
        "csd,df->csf", normed_two_all, up_full, preferred_element_type=jnp.float32
    ) + up_bias.astype(jnp.float32)
    hidden = jax.nn.gelu(hidden_pre, approximate=False).astype(jnp.bfloat16)
    mlp_terms = jnp.einsum("csf,df->csd", hidden, down_full, preferred_element_type=jnp.float32)
    mixed = lax.psum_scatter(
        mlp_terms.astype(jnp.bfloat16), "tensor", scatter_dimension=1, tiled=True
    ).astype(jnp.float32)
    output = middle + mixed + down_shift.astype(jnp.float32)
    return {
        "output": output,
        "rows": rows,
        "normed_all": normed_all,
        "queries": queries,
        "keyed": keyed,
        "valued": valued,
        "context": context,
        "log_total": log_total,
        "middle": middle,
        "normed_two_all": normed_two_all,
        "hidden_pre": hidden_pre,
        "hidden": hidden,
        "query_full": query_full,
        "key_full": key_full,
        "value_full": value_full,
        "out_full": out_full,
        "up_full": up_full,
        "down_full": down_full,
        "gain_one": gain_one,
        "bias_one": bias_one,
        "gain_two": gain_two,
        "bias_two": bias_two,
        "blocks": blocks,
    }


def local(
    tokens,
    lengths,
    cotangent,
    ln1_gain,
    ln1_bias,
    query_weight,
    query_bias,
    key_weight,
    value_weight,
    value_bias,
    out_weight,
    out_bias,
    ln2_gain,
    ln2_bias,
    up_weight,
    up_bias,
    down_weight,
    down_bias,
):
    weights = (
        ln1_gain,
        ln1_bias,
        query_weight,
        query_bias,
        key_weight,
        value_weight,
        value_bias,
        out_weight,
        out_bias,
        ln2_gain,
        ln2_bias,
        up_weight,
        up_bias,
        down_weight,
        down_bias,
    )
    saved = forward_pass(tokens, lengths, weights)
    blocks = saved["blocks"]
    grad_out = cotangent.astype(jnp.float32)
    down_shift_grad = jnp.sum(grad_out, axis=(0, 1))
    grad_out_all = lax.all_gather(cotangent, "tensor", axis=1, tiled=True)
    down_grad = jnp.einsum(
        "csd,csf->df", grad_out_all, saved["hidden"], preferred_element_type=jnp.float32
    )
    hidden_grad = jnp.einsum(
        "csd,df->csf", grad_out_all, saved["down_full"], preferred_element_type=jnp.float32
    )
    gelu_pull = jax.vjp(lambda pre: jax.nn.gelu(pre, approximate=False), saved["hidden_pre"])[1]
    pre_grad = gelu_pull(hidden_grad)[0].astype(jnp.bfloat16)
    up_shift_grad = jnp.sum(pre_grad, axis=(0, 1), dtype=jnp.float32)
    up_grad = jnp.einsum(
        "csd,csf->df", saved["normed_two_all"], pre_grad, preferred_element_type=jnp.float32
    )
    up_grad_shard, down_grad_shard = (
        lax.psum_scatter(
            up_grad.astype(jnp.bfloat16), "dp", scatter_dimension=0, tiled=True
        ).astype(jnp.float32),
        lax.psum_scatter(
            down_grad.astype(jnp.bfloat16), "dp", scatter_dimension=0, tiled=True
        ).astype(jnp.float32),
    )
    normed_two_terms = jnp.einsum(
        "csf,df->csd", pre_grad, saved["up_full"], preferred_element_type=jnp.float32
    )
    normed_two_grad = lax.psum_scatter(
        normed_two_terms.astype(jnp.bfloat16), "tensor", scatter_dimension=1, tiled=True
    ).astype(jnp.float32)
    norm_pull = jax.vjp(layer_norm, saved["middle"], saved["gain_two"], saved["bias_two"])[1]
    middle_part, gain_two_grad, bias_two_grad = norm_pull(normed_two_grad)
    middle_grad = grad_out + middle_part
    out_shift_grad = jnp.sum(middle_grad, axis=(0, 1))
    middle_all = lax.all_gather(middle_grad.astype(jnp.bfloat16), "tensor", axis=1, tiled=True)
    out_grad = jnp.einsum(
        "csd,csh->dh", middle_all, saved["context"], preferred_element_type=jnp.float32
    )
    context_grad = jnp.einsum(
        "csd,dh->csh", middle_all, saved["out_full"], preferred_element_type=jnp.float32
    ).astype(jnp.bfloat16)
    queries = saved["queries"]
    clips, seq, heads = (queries.shape[0], queries.shape[1], queries.shape[2])

    def clip_back(item):
        valid = lax.broadcasted_iota(jnp.int32, (seq,), 0) < item[5]
        return attend_back(item[0], item[1], item[2], item[3], item[4], valid, blocks)

    query_grad, key_grad, value_grad = lax.map(
        clip_back,
        (
            queries,
            saved["keyed"],
            saved["valued"],
            context_grad.reshape(clips, seq, heads, HEAD_DIM),
            saved["log_total"],
            lengths,
        ),
    )
    flat = (clips, seq, heads * HEAD_DIM)
    query_grad = query_grad.reshape(flat)
    key_grad = key_grad.reshape(flat)
    value_grad = value_grad.reshape(flat)
    normed_all = saved["normed_all"]
    query_weight_grad = jnp.einsum(
        "csd,csh->dh", normed_all, query_grad, preferred_element_type=jnp.float32
    )
    key_weight_grad = jnp.einsum(
        "csd,csh->dh", normed_all, key_grad, preferred_element_type=jnp.float32
    )
    value_weight_grad = jnp.einsum(
        "csd,csh->dh", normed_all, value_grad, preferred_element_type=jnp.float32
    )
    query_shift_grad = jnp.sum(query_grad, axis=(0, 1), dtype=jnp.float32)
    value_shift_grad = jnp.sum(value_grad, axis=(0, 1), dtype=jnp.float32)
    normed_terms = (
        jnp.einsum(
            "csh,dh->csd", query_grad, saved["query_full"], preferred_element_type=jnp.float32
        )
        + jnp.einsum("csh,dh->csd", key_grad, saved["key_full"], preferred_element_type=jnp.float32)
        + jnp.einsum(
            "csh,dh->csd", value_grad, saved["value_full"], preferred_element_type=jnp.float32
        )
    )
    normed_grad = lax.psum_scatter(
        normed_terms.astype(jnp.bfloat16), "tensor", scatter_dimension=1, tiled=True
    ).astype(jnp.float32)
    first_pull = jax.vjp(layer_norm, saved["rows"], saved["gain_one"], saved["bias_one"])[1]
    tokens_part, gain_one_grad, bias_one_grad = first_pull(normed_grad)
    tokens_grad = middle_grad + tokens_part
    summed = lax.psum(
        (
            gain_one_grad,
            bias_one_grad,
            out_shift_grad,
            gain_two_grad,
            bias_two_grad,
            down_shift_grad,
        ),
        "tensor",
    )
    owned = (
        lax.psum_scatter(
            query_weight_grad.astype(jnp.bfloat16), "dp", scatter_dimension=0, tiled=True
        ).astype(jnp.float32),
        lax.psum_scatter(
            key_weight_grad.astype(jnp.bfloat16), "dp", scatter_dimension=0, tiled=True
        ).astype(jnp.float32),
        lax.psum_scatter(
            value_weight_grad.astype(jnp.bfloat16), "dp", scatter_dimension=0, tiled=True
        ).astype(jnp.float32),
        lax.psum_scatter(
            out_grad.astype(jnp.bfloat16), "dp", scatter_dimension=0, tiled=True
        ).astype(jnp.float32),
        lax.psum_scatter(
            summed[0].astype(jnp.bfloat16), "dp", scatter_dimension=0, tiled=True
        ).astype(jnp.float32),
        lax.psum_scatter(
            summed[1].astype(jnp.bfloat16), "dp", scatter_dimension=0, tiled=True
        ).astype(jnp.float32),
        lax.psum_scatter(
            summed[2].astype(jnp.bfloat16), "dp", scatter_dimension=0, tiled=True
        ).astype(jnp.float32),
        lax.psum_scatter(
            summed[3].astype(jnp.bfloat16), "dp", scatter_dimension=0, tiled=True
        ).astype(jnp.float32),
        lax.psum_scatter(
            summed[4].astype(jnp.bfloat16), "dp", scatter_dimension=0, tiled=True
        ).astype(jnp.float32),
        lax.psum_scatter(
            summed[5].astype(jnp.bfloat16), "dp", scatter_dimension=0, tiled=True
        ).astype(jnp.float32),
    )
    shared = lax.psum((query_shift_grad, value_shift_grad, up_shift_grad), "dp")
    return (
        saved["output"].astype(jnp.bfloat16),
        tokens_grad,
        owned[4],
        owned[5],
        owned[0],
        shared[0],
        owned[1],
        owned[2],
        shared[1],
        owned[3],
        owned[6],
        owned[7],
        owned[8],
        up_grad_shard,
        shared[2],
        down_grad_shard,
        owned[9],
    )


def plane_local(
    tokens,
    lengths,
    cotangent,
    ln1_gain,
    ln1_bias,
    query_weight,
    query_bias,
    key_weight,
    value_weight,
    value_bias,
    out_weight,
    out_bias,
    ln2_gain,
    ln2_bias,
    up_weight,
    up_bias,
    down_weight,
    down_bias,
):
    planes = lax.axis_size("tensor")
    core, seat = lax.axis_index("core"), lax.axis_index("seat")
    plane = lax.axis_index("tensor")
    seat_word, core_word = seat.reshape(1), core.reshape(1)
    quarter, width = tokens.shape[1], tokens.shape[2]
    rows_of = query_weight.shape[0]
    wide = query_weight.shape[1]
    hidden_of = up_weight.shape[1] // SEATS
    low, full = jnp.bfloat16, jnp.float32
    group = ("core", "tensor")

    vectors = jnp.concatenate([ln1_gain, ln1_bias, out_bias, ln2_gain, ln2_bias, down_bias])
    head_pieces = pack_heads(
        [query_weight, key_weight, value_weight, out_weight],
        vectors.reshape(6, rows_of),
        [query_bias[None], value_bias[None], up_bias[None]],
        lengths,
        seat_word,
    )
    def split(rows):
        return rows.reshape(SEATS, -1, width)

    tokens_got = leave_seat(split(tokens[0]), seat)
    sub = tokens_got.shape[1]
    head_pieces = after(head_pieces, tokens_got)
    head_pieces = [head_pieces[0]] + [seat_swap(head_pieces[r], r) for r in range(1, SEATS)]
    rows_low = leave_plane(tokens_got, seat, plane, planes).reshape(quarter, width)
    head_pieces, rows_low = lax.optimization_barrier((jnp.stack(head_pieces), rows_low))
    heads_around = lax.all_gather(head_pieces, group, axis=0)
    tokens_near = gather_near(rows_low)
    ff_pieces = pack_hidden([up_weight, down_weight], seat_word)
    ff_pieces, tokens_near, cot_in = lax.optimization_barrier(
        (ff_pieces, tokens_near, split(cotangent[0]))
    )
    tokens_all = jnp.concatenate(gather_far(*tokens_near))
    seq = tokens_all.shape[0]
    ff_pieces = [ff_pieces[0]] + [seat_swap(ff_pieces[r], r) for r in range(1, SEATS)]
    cot_got = leave_seat(cot_in, seat)
    cot_got, heads_around, tokens_all = lax.optimization_barrier(
        (cot_got, heads_around, tokens_all)
    )
    cot_low = leave_plane(cot_got, seat, plane, planes).reshape(quarter, width)

    qkv_full, out_part, extra = assemble_weights(
        [(0, 3 * HEAD_DIM, SLOT), (3 * HEAD_DIM, HEAD_DIM, HEAD_DIM)],
        heads_around,
        seat_word,
        planes,
        EXTRA,
        FOLD,
    )
    vectors = extra[:, ::planes, :6, :rows_of].astype(full)
    gain_one, bias_one, out_shift, gain_two, bias_two, down_shift = (
        vectors[:, :, k].reshape(width) for k in range(6)
    )
    qkv_shift = jnp.pad(
        extra[0, :planes, 8, : 3 * HEAD_DIM].astype(full), ((0, 0), (0, SLOT - 3 * HEAD_DIM))
    ).reshape(planes * SLOT, 1)
    up_shift = extra[0, :planes, 9, :hidden_of].astype(full).reshape(planes * hidden_of)
    size = lax.dynamic_index_in_dim(at_index(extra, plane), core * planes, 0, keepdims=False)
    length = (8.0 * size[6, 0].astype(full) + size[6, 1].astype(full)).astype(jnp.int32)
    facts = jnp.stack([length, seat, plane])

    rows = rows_low.astype(full)
    normed_all = layer_norm(tokens_all.astype(full), gain_one, bias_one).astype(low)
    qkv = (dot(qkv_full, normed_all, (0, 1)) + qkv_shift).astype(low)
    qkv, cot_low, ff_pieces = lax.optimization_barrier((qkv, cot_low, jnp.stack(ff_pieces)))
    ff_around = lax.all_gather(ff_pieces, group, axis=0)
    cot_near = gather_near(cot_low)
    context, logs = attend(facts, qkv, planes, quarter)
    context, cot_near = lax.optimization_barrier((context, cot_near))
    cot_all = jnp.concatenate(gather_far(*cot_near))
    attended = scatter_near(*scatter_far(dot(context, out_part, (0, 1))))
    middle = rows + attended + out_shift
    normed_two = layer_norm(middle, gain_two, bias_two).astype(low)
    normed_two_near = gather_near(normed_two)
    up_full, down_full = assemble_weights(
        [(0, hidden_of, hidden_of), (hidden_of, hidden_of, hidden_of)],
        ff_around,
        seat_word,
        planes,
        0,
        1,
    )
    hidden_grad = dot(cot_all, down_full, (1, 0))
    normed_two_near, hidden_grad, up_full = lax.optimization_barrier(
        (normed_two_near, hidden_grad, up_full)
    )
    normed_two_all = jnp.concatenate(gather_far(*normed_two_near))
    hidden_pre = dot(normed_two_all, up_full, (1, 0)) + up_shift
    normal = 0.5 * (1.0 + lax.erf(hidden_pre * (0.5**0.5)))
    slope = normal + hidden_pre * (jnp.exp(-0.5 * hidden_pre * hidden_pre) * (0.5 / jnp.pi) ** 0.5)
    hidden = (hidden_pre * normal).astype(low)
    pre_grad = (hidden_grad * slope).astype(low)

    terms = dot(pre_grad, up_full, (1, 1))
    pre_grad_later = after(pre_grad, terms)
    own, across, along = scatter_far(terms)
    up_grad = dot(normed_two_all, pre_grad_later, (0, 0)).astype(low)
    up_shift_grad = jnp.sum(pre_grad_later, axis=0, dtype=full).reshape(planes, hidden_of)
    hidden_later = after(hidden, up_grad, across, along)
    down_grad = dot(cot_all, hidden_later, (0, 0)).astype(low)
    grad_out = cot_low.astype(full)

    ff_kept, ff_given = pack_grads(
        [(0, hidden_of, 0, hidden_of), (1, hidden_of, hidden_of, hidden_of)],
        2 * hidden_of,
        [up_grad, down_grad],
        core_word,
        planes,
    )
    ff_both = over_cores(ff_kept, ff_given)
    normed_two_grad, ff_both = lax.optimization_barrier(
        (scatter_near(own, across, along), ff_both)
    )
    ff_owned = lax.psum_scatter(ff_both, "tensor", scatter_dimension=0, tiled=False)
    middle_part, gain_two_grad, bias_two_grad = norm_back(middle, gain_two, normed_two_grad)
    middle_grad = grad_out + middle_part
    middle_low = middle_grad.astype(low)
    middle_near = gather_near(middle_low)
    mixed_terms = dot(after(hidden, middle_low), down_full, (1, 1))
    middle_near, mixed_terms = lax.optimization_barrier((middle_near, mixed_terms))
    middle_pieces = gather_far(*middle_near)
    middle_pieces, mixed_terms = lax.optimization_barrier((middle_pieces, mixed_terms))
    mixed = scatter_far(mixed_terms)

    context_grad = jnp.concatenate(
        [dot(out_part, piece, (0, 1)).astype(low) for piece in middle_pieces], axis=1
    )
    begun = attend_grad(facts, qkv, context_grad, logs, planes, quarter, 0, planes // 2)
    begun, mixed = lax.optimization_barrier((begun, mixed))
    mixed = scatter_near(*mixed)
    qkv_grad = attend_grad(
        facts, qkv, context_grad, logs, planes, quarter, planes // 2, planes - planes // 2, begun
    )
    qkv_grad, ff_owned = lax.optimization_barrier((qkv_grad, ff_owned))
    terms = dot(qkv_grad, qkv_full, (0, 1))
    qkv_grad_later, middle_pieces = after((qkv_grad, middle_pieces), terms)
    terms = scatter_far(terms)
    qkv_weight_grad = dot(normed_all, qkv_grad_later, (0, 1)).astype(low)
    out_grad = dot(jnp.concatenate(middle_pieces), context, (0, 1)).astype(low)
    output = (middle + mixed + down_shift).astype(low)
    terms, qkv_weight_grad, out_grad, output = lax.optimization_barrier(
        (terms, qkv_weight_grad, out_grad, output)
    )
    normed_grad = scatter_near(*terms)
    output_got = enter_plane(split(output), planes)
    qkv_shift_grad = jnp.sum(qkv_grad_later, axis=1, dtype=full).reshape(planes, SLOT)
    columns = 4 * HEAD_DIM
    sums = [gain_two_grad, bias_two_grad, jnp.sum(middle_grad, axis=0), jnp.sum(grad_out, axis=0)]
    by_owner = jnp.stack(sums).reshape(len(sums), SEATS, 2, rows_of).transpose(1, 2, 0, 3)
    shifts = jnp.stack(
        [jnp.pad(qkv_shift_grad, ((0, 0), (0, columns - SLOT))), up_shift_grad], axis=1
    )
    heads_kept, heads_given = pack_grads(
        [(0, SLOT, 0, 3 * HEAD_DIM), (1, HEAD_DIM, 3 * HEAD_DIM, HEAD_DIM)],
        columns,
        [qkv_weight_grad, out_grad],
        core_word,
        planes,
        FOLD,
        jnp.pad(by_owner, ((0, 0), (0, 0), (0, EXTRA - len(sums)), (0, columns - rows_of))),
        jnp.pad(shifts, ((0, 0), (8, EXTRA - 10), (0, 0))),
    )
    heads_both, ff_owned = lax.optimization_barrier(
        (over_cores(heads_kept, heads_given), ff_owned)
    )
    tokens_part, gain_one_grad, bias_one_grad = norm_back(rows, gain_one, normed_grad)
    tokens_grad = (middle_grad + tokens_part).astype(low)
    tokens_grad, heads_both, output_got = lax.optimization_barrier(
        (tokens_grad, heads_both, output_got)
    )
    heads_owned = lax.psum_scatter(heads_both, "tensor", scatter_dimension=0, tiled=False)
    tokens_grad_got = enter_plane(split(tokens_grad), planes)
    ones = jnp.concatenate([gain_one_grad, bias_one_grad])
    tokens_grad_got, ones = lax.optimization_barrier((tokens_grad_got, ones))
    output_home = enter_seat(output_got, seat, plane).reshape(quarter, width)
    tokens_grad_home = enter_seat(tokens_grad_got, seat, plane).reshape(quarter, width)
    ones = ones + core_swap(ones)
    for bits in (1, 2):
        ones = ones + seat_swap(ones, bits)
    for bits in (1, 2):
        ones = ones + plane_swap(ones, bits, planes)
    ones = lax.dynamic_slice_in_dim(
        ones.reshape(2, width), (2 * seat + core) * rows_of, rows_of, 1
    )

    up_home, down_home = finish_grads(
        [(0, hidden_of), (hidden_of, hidden_of)], seat_home(ff_owned, seat), seat_word, 0, 1
    )
    query_home, key_home, value_home, out_home, rest = finish_grads(
        [(k * HEAD_DIM, HEAD_DIM) for k in range(4)],
        seat_home(heads_owned, seat),
        seat_word,
        EXTRA,
        FOLD,
    )
    sums = jnp.sum(rest[:, :4, :rows_of], axis=0)
    query_shift_home = rest[:, 8, :HEAD_DIM].reshape(wide)
    value_shift_home = rest[:, 8, 2 * HEAD_DIM : 3 * HEAD_DIM].reshape(wide)
    up_shift_home = rest[:, 9, :hidden_of].reshape(SEATS * hidden_of)

    return (
        output_home[None],
        tokens_grad_home[None].astype(full),
        ones[0],
        ones[1],
        query_home,
        query_shift_home,
        key_home,
        value_home,
        value_shift_home,
        out_home,
        sums[2],
        sums[0],
        sums[1],
        up_home,
        up_shift_home,
        down_home,
        sums[3],
    )


def specs(rows, columns):
    both = (P(rows, columns, None), P(rows), P(rows, columns), P(columns))
    cube, first, matrix, second = both
    ins = (cube, first, cube, first, first, matrix, second, matrix, matrix, second, matrix)
    ins += (first, first, first, matrix, second, matrix, first)
    outs = (cube, cube, first, first, matrix, second, matrix, matrix, second, matrix)
    outs += (first, first, first, matrix, second, matrix, first)
    return ins, outs


def solution(mesh):
    step, rows = local, "dp"
    if mesh.shape["dp"] == 2 * SEATS and mesh.shape["tensor"] == SEATS:
        devices = mesh.devices.reshape(SEATS, 2, SEATS)
        step, rows, mesh = plane_local, ("seat", "core"), Mesh(devices, ("seat", "core", "tensor"))
    ins, outs = specs(rows, "tensor")
    return jax.shard_map(step, mesh=mesh, in_specs=ins, out_specs=outs, check_vma=False)
```
